512 devices in a mesh: gx: 16 (over z), gy: 8 (over x, core), gz: 4 (over y).
Axes of the slice: x: 4, y: 4, z: 16, core: 2. Of those that a mesh axis runs over, the one named last changes fastest.
Arguments:
- populations: float32 [19, 32, 64, 512], P(None, ('gy', 'gz'), 'gx'), may hold values from 0.5 to 1.5
- viscosity: float32 [32, 64, 512], P(('gy', 'gz'), 'gx'), may hold values from 0.01 to 0.3
- links: int32 [32, 64, 512], P(('gy', 'gz'), 'gx'), may hold values from 0 to 262143, as said below
- flags: int32 [32, 64, 512], P(('gy', 'gz'), 'gx'), may hold values from 0 to 2, as said below
- neighbours: int32 [32, 64, 18], P(('gy', 'gz'), 'gx'), may hold values from -1 to 63, as said below
- owners: int32 [32, 64], P(('gy', 'gz')), may hold values from 0 to 15, as said below
- slots: int32 [32, 64], P(('gy', 'gz')), may hold values from 0 to 15, as said below
- concentrations: float32 [4, 128, 64, 512], P(None, 'gx', 'gy', 'gz'), may hold values from 0.2 to 2
- diffusivity: float32 [128, 64, 512], P('gx', 'gy', 'gz'), may hold values from 0.04 to 0.12
- uptake_rate: float32 [128, 64, 512], P('gx', 'gy', 'gz'), may hold values from 0.02 to 0.2
Outputs:
- weighted_populations: float32 [19, 32, 64, 512], P(None, ('gy', 'gz'), 'gx')
- tissue_conc: float32 [4, 128, 64, 512], P(None, 'gx', 'gy', 'gz')
The draws below stay inside these ranges and needn't reach their ends.
Inputs may be any that keep to these rules, and one draw needn't show every extreme that they name: `links`: bit i - 1 is set when the link of population i into the site is open. `flags`: 0 interior site, 1 inlet site, 2 outlet site. `neighbours`: -1 where no block lies beside; the relation is mutual: if block b has N in direction k, N has b in the opposite direction; a block beside lies in the list of the same index of gx or of the one next to it. `owners`: no two of the 4 blocks on one index of gx have the same owner, and in every segment some owner receives exactly 1 from every index of gx. `slots`: distinct among the blocks of one segment with one owner.
All inputs are finite; a program needn't handle non-finite values.
Results may differ from the reference program's by a relative error of at most 0.0003.
Values sent between devices are 32-bit elements; how exact they have to be, the bound alone decides.
No kernel may reach another device: no remote copies, remote signals or barrier semaphores. Data moves between devices by JAX's collectives and lax.ppermute only.
A program may use at most 128 MiB of HBM per device.

```python
import math
import jax
import jax.numpy as jnp
import numpy as np
from jax import lax

Q = 19
SITES = 512
SPECIES = 4
FLOW_STEPS = 4
TISSUE_STEPS = 3
BLK_DEV = 4
BX = 8
BY = 8
BZ = 128
CAP = 1
OWNERS = 16
SEGS = 32
SEG_BLOCKS = 64
BRICK_SLOTS = 16
NX = 128
NY = 64
NZ = 512
N_GZ = 4


MOVING_DIRS = ((1, 0, 0), (-1, 0, 0), (0, 1, 0), (0, -1, 0), (0, 0, 1), (0, 0, -1), (1, 1, 0), (-1, -1, 0), (1, -1, 0), (-1, 1, 0), (1, 0, 1), (-1, 0, -1), (1, 0, -1), (-1, 0, 1), (0, 1, 1), (0, -1, -1), (0, 1, -1), (0, -1, 1))


def vessel_layout(key):
    base_key = jax.random.fold_in(key, 11)
    length = SEG_BLOCKS // 4
    vectors = jnp.array(MOVING_DIRS, jnp.int32)

    def one_segment(seg_key):
        local_perm = jax.vmap(lambda row_key: jax.random.permutation(row_key, BLK_DEV))(jax.random.split(seg_key, OWNERS)).astype(jnp.int32)
        order = (jnp.arange(OWNERS, dtype=jnp.int32)[:, None] * BLK_DEV + local_perm).reshape(SEG_BLOCKS)
        inverse = jnp.zeros((SEG_BLOCKS,), jnp.int32).at[order].set(jnp.arange(SEG_BLOCKS, dtype=jnp.int32))
        pos_z = order // 4
        pos_x = order % 4 // 2
        pos_y = order % 2
        target_x = pos_x[:, None] + vectors[None, :, 0]
        target_y = pos_y[:, None] + vectors[None, :, 1]
        target_z = pos_z[:, None] + vectors[None, :, 2]
        inside = (target_x >= 0) & (target_x < 2) & (target_y >= 0) & (target_y < 2) & (target_z >= 0) & (target_z < length)
        target = target_z * 4 + target_x * 2 + target_y
        beside = jnp.where(inside, inverse[jnp.clip(target, 0, SEG_BLOCKS - 1)], -1)
        third = jnp.arange(SITES, dtype=jnp.int32) % 8
        kinds = jnp.where((pos_z[:, None] == 0) & (third[None, :] == 0), 1, 0)
        kinds = jnp.where((pos_z[:, None] == length - 1) & (third[None, :] == 7), 2, kinds)
        flipped = jax.random.randint(jax.random.fold_in(seg_key, 5), (), 0, 2)
        kinds = jnp.where((kinds > 0) & (flipped == 1), 3 - kinds, kinds)
        return (beside.astype(jnp.int32), kinds.astype(jnp.int32))
    return jax.vmap(one_segment)(jax.random.split(base_key, SEGS))


def owner_layout(key):
    base_key = jax.random.fold_in(key, 31)

    def one_segment(seg_key):
        key_hot, key_turn, key_order, key_slot = jax.random.split(seg_key, 4)
        hottest = jax.random.randint(key_hot, (), 0, OWNERS)
        turns = jax.random.randint(key_turn, (OWNERS, 1), 0, OWNERS - 1)
        column = jnp.arange(BLK_DEV, dtype=jnp.int32)[None, :]
        spread_owner = (hottest + 1 + (turns + column - CAP) % (OWNERS - 1)) % OWNERS
        base_rows = jnp.where(column < CAP, hottest, spread_owner)
        orders = jax.vmap(lambda row_key: jax.random.permutation(row_key, BLK_DEV))(jax.random.split(key_order, OWNERS))
        owner_row = jnp.take_along_axis(base_rows, orders.astype(jnp.int32), axis=1).reshape(SEG_BLOCKS).astype(jnp.int32)
        matches = (owner_row[:, None] == jnp.arange(OWNERS, dtype=jnp.int32)[None, :]).astype(jnp.int32)
        ranks = jnp.sum(matches * (jnp.cumsum(matches, axis=0) - 1), axis=1)
        slot_perms = jax.vmap(lambda row_key: jax.random.permutation(row_key, BRICK_SLOTS))(jax.random.split(key_slot, OWNERS)).astype(jnp.int32)
        slot_perms = (slot_perms - slot_perms[:, :1] + BRICK_SLOTS - 1) % BRICK_SLOTS
        slot_row = slot_perms[owner_row, ranks]
        return (owner_row, slot_row.astype(jnp.int32))
    return jax.vmap(one_segment)(jax.random.split(base_key, SEGS))


def draw_links(key, part):
    bits_key = jax.random.fold_in(key, 23)
    raw = jax.random.randint(bits_key, (SEGS, SEG_BLOCKS, SITES, 18), 0, 8)
    opened = (raw != 0).astype(jnp.int32)
    powers = jnp.left_shift(jnp.ones((18,), jnp.int32), jnp.arange(18, dtype=jnp.int32))
    return jnp.sum(opened * powers, axis=-1).astype(jnp.int32)


def draw_flags(key, part):
    return vessel_layout(key)[1]


def draw_neighbours(key, part):
    return vessel_layout(key)[0]


def draw_owners(key, part):
    return owner_layout(key)[0]


def draw_slots(key, part):
    return owner_layout(key)[1]


def levels(own_key, dims, cuts, least, largest):
    def one(axis_at, blocks):
        steps = jax.random.uniform(jax.random.fold_in(jax.random.fold_in(own_key, 6), axis_at), (blocks,), jnp.float32, least / len(cuts), largest / len(cuts))
        return jnp.repeat(jnp.exp(steps), dims[axis_at] // blocks).reshape((-1,) + (1,) * (len(dims) - axis_at - 1))

    factor_of = one(*cuts[0])
    for cut in cuts[1:]:
        factor_of = factor_of * one(*cut)
    return factor_of


def setup_inputs(seed: int = 0) -> dict:
    streams_of = jax.random.split(jax.random.key(seed), 11)
    return {
        "populations": jnp.clip(0.5 + 1.0 * jax.random.uniform(streams_of[0], (Q, SEGS, SEG_BLOCKS, SITES), jnp.float32) ** levels(streams_of[0], (Q, SEGS, SEG_BLOCKS, SITES), ((1, 32), (2, 16)), -0.2, 0.2), 0.5, 1.5),
        "viscosity": jnp.clip(jnp.exp(math.log(0.3) - 3.4011974 * jax.random.uniform(streams_of[1], (SEGS, SEG_BLOCKS, SITES), jnp.float32) ** levels(streams_of[1], (SEGS, SEG_BLOCKS, SITES), ((0, 32), (1, 16)), -0.2, 0.2)), 0.01, 0.3),
        "links": draw_links(jax.random.fold_in(streams_of[10], 71), 0),
        "flags": draw_flags(jax.random.fold_in(streams_of[10], 71), 0),
        "neighbours": draw_neighbours(jax.random.fold_in(streams_of[10], 71), 0),
        "owners": draw_owners(jax.random.fold_in(streams_of[10], 71), 0),
        "slots": draw_slots(jax.random.fold_in(streams_of[10], 71), 0),
        "concentrations": jnp.clip(0.2 + 1.8 * jax.random.uniform(streams_of[7], (SPECIES, NX, NY, NZ), jnp.float32) ** levels(streams_of[7], (SPECIES, NX, NY, NZ), ((1, 16), (2, 8), (3, 4)), -0.2, 0.2), 0.2, 2.0),
        "diffusivity": jnp.clip(jnp.exp(math.log(0.12) - 1.0986123 * jax.random.uniform(streams_of[8], (NX, NY, NZ), jnp.float32) ** levels(streams_of[8], (NX, NY, NZ), ((0, 16), (1, 8), (2, 4)), -0.2, 0.2)), 0.04, 0.12),
        "uptake_rate": jnp.clip(jnp.exp(math.log(0.2) - 2.3025851 * jax.random.uniform(streams_of[9], (NX, NY, NZ), jnp.float32) ** levels(streams_of[9], (NX, NY, NZ), ((0, 16), (1, 8), (2, 4)), -0.2, 0.2)), 0.02, 0.2),
    }


LATTICE_DIRS = ((0, 0, 0), (1, 0, 0), (-1, 0, 0), (0, 1, 0), (0, -1, 0), (0, 0, 1), (0, 0, -1), (1, 1, 0), (-1, -1, 0), (1, -1, 0), (-1, 1, 0), (1, 0, 1), (-1, 0, -1), (1, 0, -1), (-1, 0, 1), (0, 1, 1), (0, -1, -1), (0, 1, -1), (0, -1, 1))
DIFFUSION_GAIN = (1.0, 0.6, 0.7, 0.35)
HALF_SATURATION = (0.3, 0.5, 0.8, 0.2)
ADVECT_GAIN = 3.0
INLET_DENSITY = 1.03
OUTLET_DENSITY = 0.97


def lattice_tables(shell):
    vectors = np.array(LATTICE_DIRS, dtype=np.int64)
    weights = np.array([1.0 / 3.0] + [1.0 / 18.0] * 6 + [1.0 / 36.0] * 12)
    opposite = [LATTICE_DIRS.index(tuple(-part_val for part_val in LATTICE_DIRS[member])) for member in range(19)]
    sites = np.arange(512)
    coords = np.stack([sites // 64, (sites // 8) % 8, sites % 8], axis=1)
    stride = np.array([64, 8, 1])
    shell_sites = sites[((coords == 0) | (coords == 7)).any(axis=1)]
    position = {}
    rim_source = []
    for member in range(1, 19):
        moved = coords + vectors[member]
        leaving = ((moved < 0) | (moved > 7)).any(axis=1)
        chosen = shell_sites if shell else sites[leaving]
        for site_id in chosen:
            position[(member, int(site_id))] = len(rim_source)
            rim_source.append(member * 512 + int(site_id))
    rim_width = -(-len(rim_source) // 128) * 128
    request_dir = []
    request_pos = []
    offsets = [0]
    counts = [0]
    selects = [sites.copy()]
    dir_maps = [np.zeros(512, np.int64)]
    arriving_masks = [np.zeros(512, bool)]
    shifts = [0]
    for member in range(1, 19):
        source = coords - vectors[member]
        arriving = ((source < 0) | (source > 7)).any(axis=1)
        select = sites.copy()
        dir_map = np.zeros(512, np.int64)
        offsets.append(len(request_dir))
        counts.append(int(arriving.sum()))
        for rank_pos, site_id in enumerate(sites[arriving]):
            block_dir = tuple(int(part_val) for part_val in (source[site_id] // 8))
            dir_index = LATTICE_DIRS.index(block_dir) - 1
            local_site = int(((source[site_id] % 8) * stride).sum())
            request_dir.append(dir_index)
            request_pos.append(position[(member, local_site)])
            select[site_id] = 512 + rank_pos
            dir_map[site_id] = dir_index
        selects.append(select)
        dir_maps.append(dir_map)
        arriving_masks.append(arriving)
        shifts.append(int((vectors[member] * stride).sum()))
    request_width = -(-len(request_dir) // 128) * 128
    request_dir = request_dir + [0] * (request_width - len(request_dir))
    request_pos = request_pos + [0] * (request_width - len(request_pos))
    return {"vectors": vectors, "weights": weights, "opposite": opposite, "rim_source": np.array(rim_source), "rim_width": rim_width, "request_dir": np.array(request_dir), "request_pos": np.array(request_pos), "offsets": offsets, "counts": counts, "selects": selects, "dir_maps": dir_maps, "arriving": arriving_masks, "shifts": shifts}


def equilibrium(density, momentum, vectors, weights):
    project = jnp.tensordot(vectors, momentum, axes=1, precision=lax.Precision.HIGHEST)
    square = jnp.sum(momentum * momentum, axis=0)
    return weights[:, None, None] * (density + 3.0 * project + 4.5 * project * project - 1.5 * square)


def collide(popul, relax, vectors, weights):
    density = jnp.sum(popul, axis=0)
    momentum = jnp.tensordot(vectors.T, popul, axes=1, precision=lax.Precision.HIGHEST)
    return popul - relax * (popul - equilibrium(density, momentum, vectors, weights))


def rim_rows(post, tables):
    block_count = post.shape[1]
    flat = jnp.transpose(post, (1, 0, 2)).reshape(block_count, 19 * 512)
    rim = jnp.take(flat, jnp.asarray(tables["rim_source"], jnp.int32), axis=1)
    return jnp.pad(rim, ((0, 0), (0, tables["rim_width"] - rim.shape[1])))


def stream(post, arrived, link_bits, beside_ids, tables):
    result = [post[0]]
    for member in range(1, 19):
        rolled = jnp.roll(post[member], tables["shifts"][member], axis=-1)
        start_col = tables["offsets"][member]
        pool = jnp.concatenate([rolled, arrived[:, start_col:start_col + tables["counts"][member]]], axis=1)
        pulled = jnp.take(pool, jnp.asarray(tables["selects"][member], jnp.int32), axis=1)
        beside = jnp.take(beside_ids, jnp.asarray(tables["dir_maps"][member], jnp.int32), axis=1) >= 0
        link_open = jnp.right_shift(link_bits, member - 1) % 2 == 1
        arriving = jnp.asarray(tables["arriving"][member])[None, :]
        opened = link_open & (beside | jnp.logical_not(arriving))
        result.append(jnp.where(opened, pulled, post[tables["opposite"][member]]))
    return jnp.stack(result)


def boundary(popul, site_flags, vectors, weights):
    momentum = jnp.tensordot(vectors.T, popul, axes=1, precision=lax.Precision.HIGHEST)
    density = jnp.where(site_flags == 1, INLET_DENSITY, OUTLET_DENSITY)
    settled = equilibrium(density, momentum, vectors, weights)
    return jnp.where(site_flags[None] > 0, settled, popul)


def shifted(field, offset):
    extent_x, extent_y, extent_z = field.shape[-3:]
    step_x, step_y, step_z = offset
    return field[..., 1 + step_x:extent_x - 1 + step_x, 1 + step_y:extent_y - 1 + step_y, 1 + step_z:extent_z - 1 + step_z]


def tissue_step(conc_ext, diff_ext, uptake_here, velocity):
    center = conc_ext[:, 1:-1, 1:-1, 1:-1]
    diff_mid = diff_ext[1:-1, 1:-1, 1:-1]
    spread = jnp.zeros_like(center)
    for offset in ((1, 0, 0), (-1, 0, 0), (0, 1, 0), (0, -1, 0), (0, 0, 1), (0, 0, -1)):
        beside_conc = shifted(conc_ext, offset)
        beside_diff = shifted(diff_ext, offset)
        spread = spread + 0.5 * (diff_mid + beside_diff) * (beside_conc - center)
    drifted = jnp.zeros_like(center)
    for axis_pos in range(3):
        unit_vec = [0, 0, 0]
        unit_vec[axis_pos] = 1
        ahead = shifted(conc_ext, tuple(unit_vec))
        behind = shifted(conc_ext, tuple(-part_val for part_val in unit_vec))
        speed_axis = ADVECT_GAIN * velocity[axis_pos]
        drifted = drifted - jnp.maximum(speed_axis, 0.0) * (center - behind) - jnp.minimum(speed_axis, 0.0) * (ahead - center)
    species_gain = jnp.array(DIFFUSION_GAIN, jnp.float32)[:, None, None, None]
    halfsat = jnp.array(HALF_SATURATION, jnp.float32)[:, None, None, None]
    uptake = uptake_here * center / (halfsat + jnp.abs(center))
    reaction = jnp.stack([-uptake[0], -uptake[1], 2.0 * uptake[1], -uptake[3]])
    return center + species_gain * spread + drifted + reaction


def reference(populations, viscosity, links, flags, neighbours, owners, slots, concentrations, diffusivity, uptake_rate):
    tables = lattice_tables(False)
    weights = jnp.asarray(tables["weights"], jnp.float32)
    vectors = jnp.asarray(tables["vectors"], jnp.float32)
    request_dir = jnp.asarray(tables["request_dir"], jnp.int32)
    request_pos = jnp.asarray(tables["request_pos"], jnp.int32)

    def segment(operands):
        pops_seg, visc_seg, link_seg, flag_seg, beside_seg = operands
        popul = pops_seg * weights[:, None, None]
        relax = 1.0 / (3.0 * visc_seg + 0.5)
        block_count = popul.shape[1]
        request_block = jnp.take(beside_seg, request_dir, axis=1)
        for turn_index in range(FLOW_STEPS):
            post = collide(popul, relax, vectors, weights)
            rim = rim_rows(post, tables)
            flat_index = jnp.clip(request_block, 0, block_count - 1) * rim.shape[1] + request_pos[None, :]
            arrived = jnp.take(rim.reshape(-1), flat_index)
            popul = stream(post, arrived, link_seg, beside_seg, tables)
            popul = boundary(popul, flag_seg, vectors, weights)
        momentum = jnp.tensordot(vectors.T, popul, axes=1, precision=lax.Precision.HIGHEST)
        return popul / weights[:, None, None], momentum

    weighted, momentum = lax.map(segment, (jnp.moveaxis(populations, 1, 0), viscosity, links, flags, neighbours))
    weighted = jnp.moveaxis(weighted, 0, 1)
    slot_x = BX // 8
    slot_y = BY // 8
    slot_z = BZ // 8
    seg_ids = jnp.arange(SEGS, dtype=jnp.int32)
    row_y = seg_ids // N_GZ
    row_z = seg_ids % N_GZ
    place_x = owners * slot_x + slots // (slot_y * slot_z)
    place_y = row_y[:, None] * slot_y + (slots // slot_z) % slot_y
    place_z = row_z[:, None] * slot_z + slots % slot_z
    values = jnp.transpose(momentum, (0, 2, 1, 3)).reshape(SEGS * SEG_BLOCKS, 3, 512)
    grid = jnp.zeros((NX // 8, NY // 8, NZ // 8, 3, 512), jnp.float32)
    grid = grid.at[place_x.reshape(-1), place_y.reshape(-1), place_z.reshape(-1)].set(values)
    velocity = grid.reshape(NX // 8, NY // 8, NZ // 8, 3, 8, 8, 8).transpose(3, 0, 4, 1, 5, 2, 6).reshape(3, NX, NY, NZ)
    diff_ext = jnp.pad(diffusivity, 1)
    conc = concentrations
    for turn_index in range(TISSUE_STEPS):
        conc_ext = jnp.pad(conc, ((0, 0), (1, 1), (1, 1), (1, 1)))
        conc = tissue_step(conc_ext, diff_ext, uptake_rate, velocity)
    return weighted, conc
```

```python
import jax
import jax.numpy as jnp
import numpy as np
from jax import lax
from jax.experimental import pallas as pl
from jax.experimental.pallas import tpu as pltpu
from jax.sharding import PartitionSpec as P

FLOW_STEPS = 4
DIRS = (
    (0, 0, 0),
    (1, 0, 0), (-1, 0, 0), (0, 1, 0), (0, -1, 0), (0, 0, 1), (0, 0, -1),
    (1, 1, 0), (-1, -1, 0), (1, -1, 0), (-1, 1, 0),
    (1, 0, 1), (-1, 0, -1), (1, 0, -1), (-1, 0, 1),
    (0, 1, 1), (0, -1, -1), (0, 1, -1), (0, -1, 1),
)
WEIGHT = (1.0 / 3.0,) + (1.0 / 18.0,) * 6 + (1.0 / 36.0,) * 12
OPP = tuple(DIRS.index(tuple(-v for v in c)) for c in DIRS)
GAIN = (1.0, 0.6, 0.7, 0.35)
HALF = (0.3, 0.5, 0.8, 0.2)
STRIDE = (64, 8, 1)
SITE = np.arange(512)
COORD = np.stack([SITE // 64, SITE // 8 % 8, SITE % 8], axis=1)
UNITS = tuple((a, s) for a in range(3) for s in (1, -1))
UNIT_POPS = tuple(tuple(i for i in range(1, 19) if DIRS[i][a] == s) for a, s in UNITS)
UNIT_SLOT = tuple(
    ((7, 5, 3, 1, 6) if a == 0 else (7, 6, 5, 4, 3))
    if s == 1
    else ((0, 2, 4, 6, 1) if a == 0 else (0, 1, 2, 3, 4))
    for a, s in UNITS
)
F32 = jnp.float32
GRID = (2, 8, 128)


def unit_of(a, s):
    return 2 * a + (0 if s == 1 else 1)


def dir_index(vec):
    return DIRS.index(tuple(vec)) - 1


def edge_unit(i):
    axes = [a for a in range(3) if DIRS[i][a]]
    return axes[1], axes[0]


class Sites:
    def __init__(self):
        sub = lax.broadcasted_iota(jnp.int32, GRID, 1)
        self.lane = lax.broadcasted_iota(jnp.int32, GRID, 2)
        self.sub = sub
        self.coord = (
            (sub & 3) * 2 + (self.lane >> 6),
            (self.lane >> 3) & 7,
            self.lane & 7,
        )
        self.cache = {}

    def plane(self, a, value):
        key = (a, value)
        if key not in self.cache:
            self.cache[key] = self.coord[a] == value
        return self.cache[key]

    def roll(self, v, n, dest):
        low = n % 128
        rows = (n - low) // 128
        lanes = SITE[dest] % 128

        def shift(x, k):
            return pltpu.roll(x, k % 8, 1) if k % 8 else x

        r = pltpu.roll(v, low, 2) if low else v
        same, carried = (lanes >= low).any(), (lanes < low).any()
        if same and carried:
            return jnp.where(self.lane >= low, shift(r, rows), shift(r, rows + 1))
        return shift(r, rows if same else rows + 1)


def moments(f):
    j = []
    for a in range(3):
        t = None
        for i in range(1, 19):
            if DIRS[i][a] == 0:
                continue
            if t is None:
                t = f[i] if DIRS[i][a] == 1 else -f[i]
            else:
                t = t + f[i] if DIRS[i][a] == 1 else t - f[i]
        j.append(t)
    return j


def equilibrium(r, j):
    base = r - 1.5 * (j[0] * j[0] + j[1] * j[1] + j[2] * j[2])
    out = [base * WEIGHT[0]] + [None] * 18
    for i in range(1, 19, 2):
        c = DIRS[i]
        p = None
        for a in range(3):
            if c[a]:
                t = j[a] if c[a] == 1 else -j[a]
                p = t if p is None else p + t
        even = base + 4.5 * (p * p)
        odd = 3.0 * p
        out[i] = WEIGHT[i] * (even + odd)
        out[i + 1] = WEIGHT[i] * (even - odd)
    return out


CODE = 38


def collide_pack(sites, f, relax, post_ref, unit_ref, base=0):
    r = f[0]
    for i in range(1, 19):
        r = r + f[i]
    feq = equilibrium(r, moments(f))
    post = [f[i] - relax * (f[i] - feq[i]) for i in range(19)]
    for i in range(19):
        post_ref[2 * i : 2 * i + 2] = post[i]
    for u, (a, s) in enumerate(UNITS):
        src = 7 if s == 1 else 0
        acc = post[UNIT_POPS[u][0]]
        for i, slot in list(zip(UNIT_POPS[u], UNIT_SLOT[u]))[1:]:
            moved = sites.roll(post[i], (slot - src) * STRIDE[a], COORD[:, a] == slot)
            acc = jnp.where(sites.plane(a, slot), moved, acc)
        unit_ref[base + 2 * u : base + 2 * u + 2] = acc


def stream(sites, me, nbr_ref, post_ref, unit_ref, left_ref, right_ref, code_ref, pool, got, base=0):
    for u in range(6):
        pool[u, 0:16] = left_ref[2 * u : 2 * u + 2].reshape(16, 128)
        pool[u, 16:32] = unit_ref[base + 2 * u : base + 2 * u + 2].reshape(16, 128)
        pool[u, 32:48] = right_ref[2 * u : 2 * u + 2].reshape(16, 128)
    first = (me - 1) * 4
    for k in range(18):
        d = DIRS[k + 1]
        i = OPP[k + 1]
        axes = [a for a in range(3) if d[a]]
        a = axes[0] if len(axes) == 1 else edge_unit(i)[0]
        u = unit_of(a, -d[a])
        for b in range(4):
            n = jnp.clip(nbr_ref[0, b, k] - first, 0, 11)
            got[k, 4 * b : 4 * b + 4] = pool[u, pl.ds(pl.multiple_of(4 * n, 4), 4), :]
    eff = code_ref[CODE + 2 : CODE + 4].astype(jnp.int32)
    f = [post_ref[0:2]]
    for i in range(1, 19):
        c = DIRS[i]
        axes = [a for a in range(3) if c[a]]
        dest = {a: (0 if c[a] == 1 else 7) for a in axes}
        at = {a: COORD[:, a] == dest[a] for a in axes}
        shift = sum(c[a] * STRIDE[a] for a in range(3))
        pulled = sites.roll(post_ref[2 * i : 2 * i + 2], shift, ~np.any([at[a] for a in axes], axis=0))
        for a in axes:
            u = unit_of(a, c[a])
            slot = UNIT_SLOT[u][UNIT_POPS[u].index(i)]
            face = [0, 0, 0]
            face[a] = -c[a]
            n = (dest[a] - slot) * STRIDE[a] + shift - c[a] * STRIDE[a]
            where = at[a].copy()
            for o in axes:
                if o != a:
                    where &= ~at[o]
            v = sites.roll(got[dir_index(face)].reshape(GRID), n, where)
            pulled = jnp.where(sites.plane(a, dest[a]), v, pulled)
        if len(axes) == 2:
            a, o = edge_unit(i)
            u = unit_of(a, c[a])
            slot = UNIT_SLOT[u][UNIT_POPS[u].index(i)]
            n = (dest[a] - slot) * STRIDE[a] + (dest[o] - (7 - dest[o])) * STRIDE[o]
            v = sites.roll(got[dir_index([-t for t in c])].reshape(GRID), n, at[a] & at[o])
            both = sites.plane(a, dest[a]) & sites.plane(o, dest[o])
            pulled = jnp.where(both, v, pulled)
        o = OPP[i]
        f.append(jnp.where((eff & (1 << (i - 1))) != 0, pulled, post_ref[2 * o : 2 * o + 2]))
    flag = eff >> 18
    feq = equilibrium(jnp.where(flag == 1, 1.03, 0.97).astype(F32), moments(f))
    edge = flag > 0
    return [jnp.where(edge, feq[i], f[i]) for i in range(19)]


def to_rows(dst, value, b_rows=4):
    for r in range(4):
        dst[pl.ds(r, 4, stride=4), :] = value[:, 128 * r : 128 * r + 128]


def slab(field, plane):
    return 12 + 3 * field + plane


def first_kernel(nbr_ref, pop_hbm, visc_hbm, link_hbm, flag_hbm, conc_hbm, diff_hbm, upt_hbm,
                 state, lo, hi,
                 rows, irows, pop_ref, visc_ref, link_ref, flag_in, sem):
    pairs = [(pop_hbm, pop_ref), (visc_hbm, visc_ref), (link_hbm, link_ref), (flag_hbm, flag_in)]
    for out, base in ((lo, 0), (hi, 5)):
        fields = [conc_hbm.at[s] for s in range(4)] + [diff_hbm, upt_hbm]
        for n, field in enumerate(fields):
            pairs.append((field.at[base : base + 3], out.at[slab(n, 0) : slab(n, 3)]))
    copies = [pltpu.make_async_copy(src, dst, sem.at[n]) for n, (src, dst) in enumerate(pairs)]
    for copy in copies:
        copy.start()
    for copy in copies:
        copy.wait()
    sites = Sites()
    f = []
    for i in range(19):
        to_rows(rows.at[i], pop_ref[i, 0])
    to_rows(rows.at[19], visc_ref[0])
    to_rows(irows.at[0], link_ref[0])
    to_rows(irows.at[1], flag_in[0])
    f = [rows[i].reshape(GRID) * np.float32(WEIGHT[i]) for i in range(19)]
    relax = 1.0 / (3.0 * rows[19].reshape(GRID) + 0.5)
    state[38:40] = relax
    group = lax.broadcasted_iota(jnp.int32, GRID, 0) * 2 + (sites.sub >> 2)
    closed = jnp.zeros(GRID, jnp.int32)
    zero = jnp.zeros(GRID, jnp.int32)
    for k in range(18):
        d = DIRS[k + 1]
        axes = [a for a in range(3) if d[a]]
        if len(axes) == 1:
            a = axes[0]
            s = -d[a]
            bits = jnp.full(GRID, 1 << (OPP[k + 1] - 1), jnp.int32)
            for i in UNIT_POPS[unit_of(a, s)]:
                others = [o for o in range(3) if o != a and DIRS[i][o]]
                if others:
                    o = others[0]
                    off = sites.plane(o, 0 if DIRS[i][o] == 1 else 7)
                    bits = bits | jnp.where(off, 0, 1 << (i - 1))
            bits = jnp.where(sites.plane(a, 0 if s == 1 else 7), bits, 0)
        else:
            i = OPP[k + 1]
            c = DIRS[i]
            a, o = axes
            at = sites.plane(a, 0 if c[a] == 1 else 7) & sites.plane(o, 0 if c[o] == 1 else 7)
            bits = jnp.where(at, 1 << (i - 1), 0)
        gone = [(nbr_ref[0, b, k] < 0).astype(jnp.int32) for b in range(4)]
        miss = jnp.where(
            group < 2,
            jnp.where(group == 0, gone[0], gone[1]),
            jnp.where(group == 2, gone[2], gone[3]),
        )
        closed = closed | jnp.where(miss != 0, bits, zero)
    code = (irows[0].reshape(GRID) & ~closed & ((1 << 18) - 1)) + (irows[1].reshape(GRID) << 18)
    state[40:42] = code.astype(F32)
    collide_pack(sites, f, relax, state, state, CODE + 4)
    lo[0:12] = state[42:54]
    hi[0:12] = state[42:54]


def step_kernel(nbr_ref, state, post_in, unit_in, left_ref, right_ref, post_ref, unit_ref, pool, got):
    sites = Sites()
    me = lax.axis_index("gx")
    f = stream(sites, me, nbr_ref, post_in, unit_in, left_ref, right_ref, state, pool, got)
    collide_pack(sites, f, state[CODE : CODE + 2], post_ref, unit_ref)


def second_kernel(nbr_ref, state, left_ref, right_ref, conc, diff,
                  post_ref, unit_ref, ya, yb, za, zb, pool, got):
    sites = Sites()
    me = lax.axis_index("gx")
    f = stream(sites, me, nbr_ref, state, state, left_ref, right_ref, state, pool, got, CODE + 4)
    collide_pack(sites, f, state[CODE : CODE + 2], post_ref, unit_ref)
    first_rims(conc, diff, left_ref, right_ref, ya, yb, za, zb)


def last_kernel(nbr_ref, own_ref, state, post_in, unit_in, left_ref, right_ref, out_ref, send_ref, pool, got, rows, jrows):
    sites = Sites()
    me = lax.axis_index("gx")
    f = stream(sites, me, nbr_ref, post_in, unit_in, left_ref, right_ref, state, pool, got)
    for i in range(19):
        rows[i] = (f[i] * np.float32(1.0 / WEIGHT[i])).reshape(16, 128)
    j = moments(f)
    for a in range(3):
        v = j[a]
        for bit in (8, 16, 32, 64):
            up = pltpu.roll(v, bit, 2)
            down = up if bit == 64 else pltpu.roll(v, 128 - bit, 2)
            v = jnp.where((sites.lane & bit) != 0, up, down)
        jrows[a] = v.reshape(16, 128)
    send_ref[...] = jnp.zeros(send_ref.shape, F32)
    for b in range(4):
        o = own_ref[0, 4 * me + b]
        for a in range(3):
            send_ref[o, 4 * a : 4 * a + 4] = jrows[a, 4 * b : 4 * b + 4]

        @pl.when(o < 15)
        def _():
            for a in range(3):
                send_ref[o + 1, 12 + a : 13 + a] = jrows[a, 4 * b + 3 : 4 * b + 4]

        @pl.when(o > 0)
        def _():
            for a in range(3):
                send_ref[o - 1, 15 + a : 16 + a] = jrows[a, 4 * b : 4 * b + 1]

    for i in range(19):
        for r in range(4):
            out_ref[i, 0, :, 128 * r : 128 * r + 128] = rows[i, pl.ds(r, 4, stride=4), :]


def even(axis):
    return lax.rem(lax.axis_index(axis), 2) == 0


class Rims:
    def __init__(self, lane, ya, yb):
        self.lane, self.ya, self.yb = lane, ya, yb
        self.lo = jnp.zeros((8, 128), F32)
        self.hi = jnp.zeros((8, 128), F32)
        self.y_even = even("gy")

    def put(self, value, j, s, row):
        self.ya[s, row : row + 1] = jnp.where(self.y_even, value[7:8], value[0:1])
        self.yb[s, row : row + 1] = jnp.where(self.y_even, value[0:1], value[7:8])
        at = self.lane == j
        self.lo = jnp.where(at, pltpu.roll(value, j, 1) if j else value, self.lo)
        self.hi = jnp.where(at, pltpu.roll(value, (j + 1) % 128, 1), self.hi)

    def finish(self, za, zb):
        z_even = even("gz")
        za[...] = jnp.where(z_even, self.hi, self.lo)
        zb[...] = jnp.where(z_even, self.lo, self.hi)


def first_rims(conc, diff, xl, xr, ya, yb, za, zb):
    lane = lax.broadcasted_iota(jnp.int32, (8, 128), 1)
    rims = Rims(lane, ya, yb)
    for fld in range(5):
        for p in range(12):
            q = p - 2
            if q < 0:
                v = xl[slab(fld, 3 + q)]
            elif q > 7:
                v = xr[slab(fld, q - 8)]
            else:
                v = conc[fld, q] if fld < 4 else diff[q]
            rims.put(v, fld * 12 + p, fld, p)
    rims.finish(za, zb)


class Planes:
    def __init__(self, ya, yb, za, zb):
        self.sub = lax.broadcasted_iota(jnp.int32, (8, 128), 0)
        self.lane = lax.broadcasted_iota(jnp.int32, (8, 128), 1)
        self.ya, self.yb, self.y_even = ya, yb, even("gy")
        z_even = even("gz")
        self.z_lo = jnp.where(z_even, zb[...], za[...])
        self.z_hi = jnp.where(z_even, za[...], zb[...])

    def beside(self, v, s, row, j):
        a, b = self.ya[s, row : row + 1], self.yb[s, row : row + 1]
        lo = jnp.broadcast_to(jnp.where(self.y_even, b, a), (8, 128))
        hi = jnp.broadcast_to(jnp.where(self.y_even, a, b), (8, 128))
        ym = jnp.where(self.sub == 0, lo, pltpu.roll(v, 1, 0))
        yp = jnp.where(self.sub == 7, hi, pltpu.roll(v, 7, 0))
        zl = pltpu.roll(self.z_lo, (128 - j) % 128, 1) if j else self.z_lo
        zm = jnp.where(self.lane == 0, zl, pltpu.roll(v, 1, 1))
        zp = jnp.where(self.lane == 127, pltpu.roll(self.z_hi, 127 - j, 1), pltpu.roll(v, 127, 1))
        return ym, yp, zm, zp


def advance(s, cm, c, cp, around, spread, drift, upt, up1):
    k = GAIN[s]
    acc = c
    for v, g, d in zip((cm, cp) + tuple(around), spread, drift):
        w = d + (g if k == 1.0 else k * g)
        acc = acc + w * (v - c)
    if s == 2:
        return acc + 2.0 * up1
    return acc - upt * c / (HALF[s] + jnp.abs(c))


def tissue(planes, lo, hi, get_c, get_coef, get_upt, me, store, rims=None, rim_lo=0, rim_hi=0):
    for p in range(lo, hi):
        spread, drift = get_coef(p)
        upt = get_upt(p)
        keep = me > 0 if p < 0 else (me < 15 if p > 7 else None)
        c1 = get_c(1, p)
        up1 = upt * c1 / (HALF[1] + jnp.abs(c1))
        for s in range(4):
            c = get_c(s, p)
            around = planes.beside(c, s, p - lo, s * (hi - lo) + p - lo)
            v = advance(s, get_c(s, p - 1), c, get_c(s, p + 1), around, spread, drift, upt, up1)
            if keep is not None:
                v = jnp.where(keep, v, 0.0)
            store(s, p, v)
            if rim_lo <= p < rim_hi:
                rims.put(v, s * (rim_hi - rim_lo) + p - rim_lo, s, p - rim_lo)


def velocity_kernel(own_ref, slot_ref, recv, drift, blocks, slabs):
    me = lax.axis_index("gx")
    blocks[...] = jnp.zeros(blocks.shape, F32)
    slabs[...] = jnp.zeros(slabs.shape, F32)
    for m in range(16):
        own, low, high = jnp.int32(16), jnp.int32(16), jnp.int32(16)
        for b in range(4):
            o = own_ref[0, 4 * m + b]
            at = slot_ref[0, 4 * m + b]
            own = jnp.where(o == me, at, own)
            low = jnp.where(o == me - 1, at, low)
            high = jnp.where(o == me + 1, at, high)
        blocks[pl.ds(pl.multiple_of(16 * own, 16), 16), :] = recv[m, 0:16]
        for a in range(3):
            slabs[a, pl.ds(low, 1), :] = recv[m, 12 + a : 13 + a]
            slabs[3 + a, pl.ds(high, 1), :] = recv[m, 15 + a : 16 + a]
    group = lax.broadcasted_iota(jnp.int32, (16, 128), 1) >> 3
    masks = [(group & (1 << bit)) != 0 for bit in range(4)]

    def turned(x):
        x = pltpu.roll(x, 8, 1, stride=8, stride_axis=0)
        for bit in range(4):
            x = jnp.where(masks[bit], pltpu.roll(x, 16 - (1 << bit), 0), x)
        return pltpu.roll(x, 0, 1, stride=8, stride_axis=0)

    for a in range(3):
        for r in range(6):
            if r == 0:
                x = slabs[a, 0:16]
            elif r == 5:
                x = slabs[3 + a, 0:16]
            else:
                x = blocks[pl.ds(4 * a + r - 1, 16, stride=16), :]
            t = turned(x)
            for h in range(2):
                u = 3.0 * t[8 * h : 8 * h + 8]
                drift[2 * a, 2 * r + h] = jnp.maximum(u, 0.0)
                drift[2 * a + 1, 2 * r + h] = -jnp.minimum(u, 0.0)


def tissue1_kernel(drift, conc, diff, upt, xl, xr, za, zb, ya, yb,
                   c_out, spread_out, y0, y1, z0, z1):
    me = lax.axis_index("gx")
    planes = Planes(ya, yb, za, zb)

    def field(f, own):
        def get(p):
            if p < 0:
                return xl[slab(f, 3 + p)]
            if p > 7:
                return xr[slab(f, p - 8)]
            return own(p)
        return get

    get_d = field(4, lambda p: diff[p])
    get_u = field(5, lambda p: upt[p])
    gets = [field(s, lambda p, s=s: conc[s, p]) for s in range(4)]

    def get_coef(p):
        d = get_d(p)
        q = p + 2
        around = planes.beside(d, 4, q, 48 + q)
        spread = [0.5 * (d + n) for n in (get_d(p - 1), get_d(p + 1)) + tuple(around)]
        for n in range(6):
            spread_out[n, q] = spread[n]
        return spread, [drift[n, q] for n in range(6)]

    def store(s, p, v):
        c_out[s, p + 2] = v

    rims = Rims(planes.lane, y0, y1)
    tissue(planes, -2, 10, lambda s, p: gets[s](p), get_coef, get_u, me, store, rims, -1, 9)
    rims.finish(z0, z1)


def later_coef(spread, drift):
    return lambda p: ([spread[n, p + 2] for n in range(6)], [drift[n, p + 2] for n in range(6)])


def tissue2_kernel(drift, spread, conc, upt, xl, xr, za, zb, ya, yb, c_out, y0, y1, z0, z1):
    me = lax.axis_index("gx")
    planes = Planes(ya, yb, za, zb)

    def get_u(p):
        return xl[slab(5, 3 + p)] if p < 0 else (xr[slab(5, p - 8)] if p > 7 else upt[p])

    def store(s, p, v):
        c_out[s, p + 1] = v

    rims = Rims(planes.lane, y0, y1)
    tissue(planes, -1, 9, lambda s, p: conc[s, p + 2], later_coef(spread, drift), get_u, me, store,
           rims, 0, 8)
    rims.finish(z0, z1)


def tissue3_kernel(drift, spread, conc, upt, za, zb, ya, yb, out):
    planes = Planes(ya, yb, za, zb)

    def store(s, p, v):
        out[s, p] = v

    tissue(planes, 0, 8, lambda s, p: conc[s, p + 1], later_coef(spread, drift), lambda p: upt[p],
           None, store)


VMEM = pltpu.VMEM


def call(kernel, smem, arrays, outs, scratch=(), space=VMEM, limit=8 << 20):
    return pl.pallas_call(
        kernel,
        in_specs=[pl.BlockSpec(memory_space=pltpu.SMEM)] * len(smem)
        + [pl.BlockSpec(memory_space=space)] * len(arrays),
        out_specs=tuple(pl.BlockSpec(memory_space=VMEM) for _ in outs),
        out_shape=tuple(jax.ShapeDtypeStruct(s, t) for s, t in outs),
        scratch_shapes=[VMEM(*x) if isinstance(x, tuple) else x for x in scratch],
        compiler_params=pltpu.CompilerParams(vmem_limit_bytes=limit),
        name=kernel.__name__,
    )(*smem, *arrays)


def hop(x, axis, step):
    n = lax.axis_size(axis)
    return lax.ppermute(x, axis, [(i, i + step) for i in range(n) if 0 <= i + step < n])


def swap(x, axis, first):
    n = lax.axis_size(axis)
    return lax.ppermute(x, axis, [(i, j) for i in range(n) for j in [i ^ 1 if first else ((i + 1) ^ 1) - 1] if 0 <= j < n])


def swaps(turn, ya, yb, za, zb):
    out = []
    for name, x, axis, first in (("za", za, "gz", True), ("zb", zb, "gz", False), ("ya", ya, "gy", True), ("yb", yb, "gy", False)):
        with jax.named_scope(f"{name}{turn}"):
            out.append(swap(x, axis, first))
    return tuple(out)


def shards(populations, viscosity, links, flags, neighbours, owners, slots, conc, diff, upt):
    i32 = jnp.int32
    tiles = lambda n: ((n, 8, 128), F32)
    tile = ((8, 128), F32)
    faces = lambda fields, rows: [((fields, rows, 128), F32)] * 2 + [tile, tile]
    pool = [((6, 48, 128), F32), ((18, 16, 128), F32)]
    state, lo, hi = call(
        first_kernel, (neighbours,), (populations, viscosity, links, flags, conc, diff, upt),
        [tiles(54), tiles(30), tiles(30)],
        [((20, 16, 128), F32), ((2, 16, 128), i32), ((19, 1, 4, 512), F32), ((1, 4, 512), F32),
         ((1, 4, 512), i32), ((1, 4, 512), i32), pltpu.SemaphoreType.DMA((16,))],
        space=pltpu.HBM, limit=67043328 - (420 << 10),
    )
    xl, xr = hop(hi, "gx", 1), hop(lo, "gx", -1)
    post, unit, *rim = call(
        second_kernel, (neighbours,), (state, xl, xr, conc, diff),
        [tiles(38), tiles(12)] + faces(5, 16), pool,
    )
    rim = swaps(0, *rim)
    for _ in range(FLOW_STEPS - 2):
        left, right = hop(unit, "gx", 1), hop(unit, "gx", -1)
        post, unit = call(
            step_kernel, (neighbours,), (state, post, unit, left, right), [tiles(38), tiles(12)], pool
        )
    left, right = hop(unit, "gx", 1), hop(unit, "gx", -1)
    weighted, send = call(
        last_kernel, (neighbours, owners), (state, post, unit, left, right),
        [((19, 1, 4, 512), F32), ((16, 24, 128), F32)],
        pool + [((19, 16, 128), F32), ((3, 16, 128), F32)],
    )
    with jax.named_scope("spread"):
        recv = lax.all_to_all(send, "gx", 0, 0)
    with jax.named_scope("drift"):
        (drift,) = call(
            velocity_kernel, (owners, slots), (recv,), [((6, 12, 8, 128), F32)],
            [((17 * 16, 128), F32), ((6, 24, 128), F32)],
        )
    c1, spread, *faces1 = call(
        tissue1_kernel, (), (drift, conc, diff, upt, xl, xr) + rim,
        [((4, 12, 8, 128), F32), ((6, 12, 8, 128), F32)] + faces(4, 16),
    )
    c2, *faces2 = call(
        tissue2_kernel, (), (drift, spread, c1, upt, xl, xr) + swaps(1, *faces1),
        [((4, 10, 8, 128), F32)] + faces(4, 8),
    )
    (out,) = call(
        tissue3_kernel, (), (drift, spread, c2, upt) + swaps(2, *faces2), [((4, 8, 8, 128), F32)]
    )
    return weighted, out


def solution(mesh):
    site = P(("gy", "gz"), "gx", None)
    brick = P("gx", "gy", "gz")
    return jax.shard_map(
        shards,
        mesh=mesh,
        in_specs=(
            P(None, ("gy", "gz"), "gx", None), site, site, site, site,
            P(("gy", "gz"), None), P(("gy", "gz"), None),
            P(None, "gx", "gy", "gz"), brick, brick,
        ),
        out_specs=(P(None, ("gy", "gz"), "gx", None), P(None, "gx", "gy", "gz")),
        check_vma=False,
    )
```

```python
import jax
import jax.numpy as jnp
import numpy as np
from jax import lax
from jax.experimental import pallas as pl
from jax.experimental.pallas import tpu as pltpu
from jax.sharding import PartitionSpec as P

FLOW_STEPS = 4
DIRS = (
    (0, 0, 0),
    (1, 0, 0), (-1, 0, 0), (0, 1, 0), (0, -1, 0), (0, 0, 1), (0, 0, -1),
    (1, 1, 0), (-1, -1, 0), (1, -1, 0), (-1, 1, 0),
    (1, 0, 1), (-1, 0, -1), (1, 0, -1), (-1, 0, 1),
    (0, 1, 1), (0, -1, -1), (0, 1, -1), (0, -1, 1),
)
WEIGHT = (1.0 / 3.0,) + (1.0 / 18.0,) * 6 + (1.0 / 36.0,) * 12
OPP = tuple(DIRS.index(tuple(-v for v in c)) for c in DIRS)
GAIN = (1.0, 0.6, 0.7, 0.35)
HALF = (0.3, 0.5, 0.8, 0.2)
STRIDE = (64, 8, 1)
SITE = np.arange(512)
COORD = np.stack([SITE // 64, SITE // 8 % 8, SITE % 8], axis=1)
UNITS = tuple((a, s) for a in range(3) for s in (1, -1))
UNIT_POPS = tuple(tuple(i for i in range(1, 19) if DIRS[i][a] == s) for a, s in UNITS)
UNIT_SLOT = tuple(
    ((7, 5, 3, 1, 6) if a == 0 else (7, 6, 5, 4, 3))
    if s == 1
    else ((0, 2, 4, 6, 1) if a == 0 else (0, 1, 2, 3, 4))
    for a, s in UNITS
)
F32 = jnp.float32
GRID = (2, 8, 128)


def unit_of(a, s):
    return 2 * a + (0 if s == 1 else 1)


def dir_index(vec):
    return DIRS.index(tuple(vec)) - 1


def edge_unit(i):
    axes = [a for a in range(3) if DIRS[i][a]]
    return axes[1], axes[0]


class Sites:
    def __init__(self):
        sub = lax.broadcasted_iota(jnp.int32, GRID, 1)
        self.lane = lax.broadcasted_iota(jnp.int32, GRID, 2)
        self.sub = sub
        self.coord = (
            (sub & 3) * 2 + (self.lane >> 6),
            (self.lane >> 3) & 7,
            self.lane & 7,
        )
        self.cache = {}

    def plane(self, a, value):
        key = (a, value)
        if key not in self.cache:
            self.cache[key] = self.coord[a] == value
        return self.cache[key]

    def roll(self, v, n, dest):
        low = n % 128
        rows = (n - low) // 128
        lanes = SITE[dest] % 128

        def shift(x, k):
            return pltpu.roll(x, k % 8, 1) if k % 8 else x

        r = pltpu.roll(v, low, 2) if low else v
        same, carried = (lanes >= low).any(), (lanes < low).any()
        if same and carried:
            return jnp.where(self.lane >= low, shift(r, rows), shift(r, rows + 1))
        return shift(r, rows if same else rows + 1)


def moments(f):
    j = []
    for a in range(3):
        t = None
        for i in range(1, 19):
            if DIRS[i][a] == 0:
                continue
            if t is None:
                t = f[i] if DIRS[i][a] == 1 else -f[i]
            else:
                t = t + f[i] if DIRS[i][a] == 1 else t - f[i]
        j.append(t)
    return j


def equilibrium(r, j):
    base = r - 1.5 * (j[0] * j[0] + j[1] * j[1] + j[2] * j[2])
    out = [base * WEIGHT[0]] + [None] * 18
    for i in range(1, 19, 2):
        c = DIRS[i]
        p = None
        for a in range(3):
            if c[a]:
                t = j[a] if c[a] == 1 else -j[a]
                p = t if p is None else p + t
        even = base + 4.5 * (p * p)
        odd = 3.0 * p
        out[i] = WEIGHT[i] * (even + odd)
        out[i + 1] = WEIGHT[i] * (even - odd)
    return out


CODE = 38


def collide_pack(sites, f, relax, post_ref, unit_ref, base=0):
    r = f[0]
    for i in range(1, 19):
        r = r + f[i]
    feq = equilibrium(r, moments(f))
    post = [f[i] - relax * (f[i] - feq[i]) for i in range(19)]
    for i in range(19):
        post_ref[2 * i : 2 * i + 2] = post[i]
    for u, (a, s) in enumerate(UNITS):
        src = 7 if s == 1 else 0
        acc = post[UNIT_POPS[u][0]]
        for i, slot in list(zip(UNIT_POPS[u], UNIT_SLOT[u]))[1:]:
            moved = sites.roll(post[i], (slot - src) * STRIDE[a], COORD[:, a] == slot)
            acc = jnp.where(sites.plane(a, slot), moved, acc)
        unit_ref[base + 2 * u : base + 2 * u + 2] = acc


def stream(sites, me, nbr_ref, post_ref, unit_ref, left_ref, right_ref, code_ref, pool, got, base=0):
    for u in range(6):
        pool[u, 0:16] = left_ref[2 * u : 2 * u + 2].reshape(16, 128)
        pool[u, 16:32] = unit_ref[base + 2 * u : base + 2 * u + 2].reshape(16, 128)
        pool[u, 32:48] = right_ref[2 * u : 2 * u + 2].reshape(16, 128)
    first = (me - 1) * 4
    for k in range(18):
        d = DIRS[k + 1]
        i = OPP[k + 1]
        axes = [a for a in range(3) if d[a]]
        a = axes[0] if len(axes) == 1 else edge_unit(i)[0]
        u = unit_of(a, -d[a])
        for b in range(4):
            n = jnp.clip(nbr_ref[0, b, k] - first, 0, 11)
            got[k, 4 * b : 4 * b + 4] = pool[u, pl.ds(pl.multiple_of(4 * n, 4), 4), :]
    eff = code_ref[CODE + 2 : CODE + 4].astype(jnp.int32)
    f = [post_ref[0:2]]
    for i in range(1, 19):
        c = DIRS[i]
        axes = [a for a in range(3) if c[a]]
        dest = {a: (0 if c[a] == 1 else 7) for a in axes}
        at = {a: COORD[:, a] == dest[a] for a in axes}
        shift = sum(c[a] * STRIDE[a] for a in range(3))
        pulled = sites.roll(post_ref[2 * i : 2 * i + 2], shift, ~np.any([at[a] for a in axes], axis=0))
        for a in axes:
            u = unit_of(a, c[a])
            slot = UNIT_SLOT[u][UNIT_POPS[u].index(i)]
            face = [0, 0, 0]
            face[a] = -c[a]
            n = (dest[a] - slot) * STRIDE[a] + shift - c[a] * STRIDE[a]
            where = at[a].copy()
            for o in axes:
                if o != a:
                    where &= ~at[o]
            v = sites.roll(got[dir_index(face)].reshape(GRID), n, where)
            pulled = jnp.where(sites.plane(a, dest[a]), v, pulled)
        if len(axes) == 2:
            a, o = edge_unit(i)
            u = unit_of(a, c[a])
            slot = UNIT_SLOT[u][UNIT_POPS[u].index(i)]
            n = (dest[a] - slot) * STRIDE[a] + (dest[o] - (7 - dest[o])) * STRIDE[o]
            v = sites.roll(got[dir_index([-t for t in c])].reshape(GRID), n, at[a] & at[o])
            both = sites.plane(a, dest[a]) & sites.plane(o, dest[o])
            pulled = jnp.where(both, v, pulled)
        o = OPP[i]
        f.append(jnp.where((eff & (1 << (i - 1))) != 0, pulled, post_ref[2 * o : 2 * o + 2]))
    flag = eff >> 18
    feq = equilibrium(jnp.where(flag == 1, 1.03, 0.97).astype(F32), moments(f))
    edge = flag > 0
    return [jnp.where(edge, feq[i], f[i]) for i in range(19)]


def to_rows(dst, value, b_rows=4):
    for r in range(4):
        dst[pl.ds(r, 4, stride=4), :] = value[:, 128 * r : 128 * r + 128]


def slab(field, plane):
    return 12 + 3 * field + plane


def first_kernel(nbr_ref, pop_hbm, visc_hbm, link_hbm, flag_hbm, conc_hbm, diff_hbm, upt_hbm,
                 state, lo, hi,
                 rows, irows, pop_ref, visc_ref, link_ref, flag_in, sem):
    pairs = [(pop_hbm, pop_ref), (visc_hbm, visc_ref), (link_hbm, link_ref), (flag_hbm, flag_in)]
    for out, base in ((lo, 0), (hi, 5)):
        fields = [conc_hbm.at[s] for s in range(4)] + [diff_hbm, upt_hbm]
        for n, field in enumerate(fields):
            pairs.append((field.at[base : base + 3], out.at[slab(n, 0) : slab(n, 3)]))
    copies = [pltpu.make_async_copy(src, dst, sem.at[n]) for n, (src, dst) in enumerate(pairs)]
    for copy in copies:
        copy.start()
    for copy in copies:
        copy.wait()
    sites = Sites()
    f = []
    for i in range(19):
        to_rows(rows.at[i], pop_ref[i, 0])
    to_rows(rows.at[19], visc_ref[0])
    to_rows(irows.at[0], link_ref[0])
    to_rows(irows.at[1], flag_in[0])
    f = [rows[i].reshape(GRID) * np.float32(WEIGHT[i]) for i in range(19)]
    relax = 1.0 / (3.0 * rows[19].reshape(GRID) + 0.5)
    state[38:40] = relax
    group = lax.broadcasted_iota(jnp.int32, GRID, 0) * 2 + (sites.sub >> 2)
    closed = jnp.zeros(GRID, jnp.int32)
    zero = jnp.zeros(GRID, jnp.int32)
    for k in range(18):
        d = DIRS[k + 1]
        axes = [a for a in range(3) if d[a]]
        if len(axes) == 1:
            a = axes[0]
            s = -d[a]
            bits = jnp.full(GRID, 1 << (OPP[k + 1] - 1), jnp.int32)
            for i in UNIT_POPS[unit_of(a, s)]:
                others = [o for o in range(3) if o != a and DIRS[i][o]]
                if others:
                    o = others[0]
                    off = sites.plane(o, 0 if DIRS[i][o] == 1 else 7)
                    bits = bits | jnp.where(off, 0, 1 << (i - 1))
            bits = jnp.where(sites.plane(a, 0 if s == 1 else 7), bits, 0)
        else:
            i = OPP[k + 1]
            c = DIRS[i]
            a, o = axes
            at = sites.plane(a, 0 if c[a] == 1 else 7) & sites.plane(o, 0 if c[o] == 1 else 7)
            bits = jnp.where(at, 1 << (i - 1), 0)
        gone = [(nbr_ref[0, b, k] < 0).astype(jnp.int32) for b in range(4)]
        miss = jnp.where(
            group < 2,
            jnp.where(group == 0, gone[0], gone[1]),
            jnp.where(group == 2, gone[2], gone[3]),
        )
        closed = closed | jnp.where(miss != 0, bits, zero)
    code = (irows[0].reshape(GRID) & ~closed & ((1 << 18) - 1)) + (irows[1].reshape(GRID) << 18)
    state[40:42] = code.astype(F32)
    collide_pack(sites, f, relax, state, state, CODE + 4)
    lo[0:12] = state[42:54]
    hi[0:12] = state[42:54]


def step_kernel(nbr_ref, state, post_in, unit_in, left_ref, right_ref, post_ref, unit_ref, pool, got):
    sites = Sites()
    me = lax.axis_index("gx")
    f = stream(sites, me, nbr_ref, post_in, unit_in, left_ref, right_ref, state, pool, got)
    collide_pack(sites, f, state[CODE : CODE + 2], post_ref, unit_ref)


def second_kernel(nbr_ref, state, left_ref, right_ref, conc, diff,
                  post_ref, unit_ref, ya, yb, za, zb, pool, got):
    sites = Sites()
    me = lax.axis_index("gx")
    f = stream(sites, me, nbr_ref, state, state, left_ref, right_ref, state, pool, got, CODE + 4)
    collide_pack(sites, f, state[CODE : CODE + 2], post_ref, unit_ref)
    first_rims(conc, diff, left_ref, right_ref, ya, yb, za, zb)


def last_kernel(nbr_ref, own_ref, state, post_in, unit_in, left_ref, right_ref, out_ref, send_ref, pool, got, rows, jrows):
    sites = Sites()
    me = lax.axis_index("gx")
    f = stream(sites, me, nbr_ref, post_in, unit_in, left_ref, right_ref, state, pool, got)
    for i in range(19):
        rows[i] = (f[i] * np.float32(1.0 / WEIGHT[i])).reshape(16, 128)
    j = moments(f)
    for a in range(3):
        v = j[a]
        for bit in (8, 16, 32, 64):
            up = pltpu.roll(v, bit, 2)
            down = up if bit == 64 else pltpu.roll(v, 128 - bit, 2)
            v = jnp.where((sites.lane & bit) != 0, up, down)
        jrows[a] = v.reshape(16, 128)
    send_ref[...] = jnp.zeros(send_ref.shape, F32)
    for b in range(4):
        o = own_ref[0, 4 * me + b]
        for a in range(3):
            send_ref[o, 4 * a : 4 * a + 4] = jrows[a, 4 * b : 4 * b + 4]

        @pl.when(o < 15)
        def _():
            for a in range(3):
                send_ref[o + 1, 12 + a : 13 + a] = jrows[a, 4 * b + 3 : 4 * b + 4]

        @pl.when(o > 0)
        def _():
            for a in range(3):
                send_ref[o - 1, 15 + a : 16 + a] = jrows[a, 4 * b : 4 * b + 1]

    for i in range(19):
        for r in range(4):
            out_ref[i, 0, :, 128 * r : 128 * r + 128] = rows[i, pl.ds(r, 4, stride=4), :]


def even(axis):
    return lax.rem(lax.axis_index(axis), 2) == 0


class Rims:
    def __init__(self, lane, ya, yb):
        self.lane, self.ya, self.yb = lane, ya, yb
        self.lo = jnp.zeros((8, 128), F32)
        self.hi = jnp.zeros((8, 128), F32)
        self.y_even = even("gy")

    def put(self, value, j, s, row):
        self.ya[s, row : row + 1] = jnp.where(self.y_even, value[7:8], value[0:1])
        self.yb[s, row : row + 1] = jnp.where(self.y_even, value[0:1], value[7:8])
        at = self.lane == j
        self.lo = jnp.where(at, pltpu.roll(value, j, 1) if j else value, self.lo)
        self.hi = jnp.where(at, pltpu.roll(value, (j + 1) % 128, 1), self.hi)

    def finish(self, za, zb):
        z_even = even("gz")
        za[...] = jnp.where(z_even, self.hi, self.lo)
        zb[...] = jnp.where(z_even, self.lo, self.hi)


def first_rims(conc, diff, xl, xr, ya, yb, za, zb):
    lane = lax.broadcasted_iota(jnp.int32, (8, 128), 1)
    rims = Rims(lane, ya, yb)
    for fld in range(5):
        for p in range(12):
            q = p - 2
            if q < 0:
                v = xl[slab(fld, 3 + q)]
            elif q > 7:
                v = xr[slab(fld, q - 8)]
            else:
                v = conc[fld, q] if fld < 4 else diff[q]
            rims.put(v, fld * 12 + p, fld, p)
    rims.finish(za, zb)


def beside(v, lo, hi, z_lo, z_hi, j):
    sub = lax.broadcasted_iota(jnp.int32, (8, 128), 0)
    lane = lax.broadcasted_iota(jnp.int32, (8, 128), 1)
    ym = jnp.where(sub == 0, jnp.broadcast_to(lo, (8, 128)), pltpu.roll(v, 1, 0))
    yp = jnp.where(sub == 7, jnp.broadcast_to(hi, (8, 128)), pltpu.roll(v, 7, 0))
    return (ym, yp) + beside_z(v, z_lo, z_hi, j, j)


def beside_z(v, z_lo, z_hi, j_lo, j_hi):
    lane = lax.broadcasted_iota(jnp.int32, (8, 128), 1)
    zm = jnp.where(lane == 0, turn(z_lo, -j_lo), pltpu.roll(v, 1, 1))
    zp = jnp.where(lane == 127, turn(z_hi, 127 - j_hi), pltpu.roll(v, 127, 1))
    return zm, zp


def turn(v, n):
    return pltpu.roll(v, n % 128, 1) if n % 128 else v


def advance(s, cm, c, cp, around, spread, drift, upt, up1):
    k = GAIN[s]
    acc = c
    for v, g, d in zip((cm, cp) + tuple(around), spread, drift):
        w = d + (g if k == 1.0 else k * g)
        acc = acc + w * (v - c)
    if s == 2:
        return acc + 2.0 * up1
    return acc - upt * c / (HALF[s] + jnp.abs(c))


def tissue(lo, hi, get_c, around, get_coef, get_upt, me, store):
    for p in range(lo, hi):
        spread, drift = get_coef(p)
        upt = get_upt(p)
        keep = me > 0 if p < 0 else (me < 15 if p > 7 else None)
        c1 = get_c(1, p)
        up1 = upt * c1 / (HALF[1] + jnp.abs(c1))
        for s in range(4):
            c = get_c(s, p)
            v = advance(s, get_c(s, p - 1), c, get_c(s, p + 1), around(s, p, c), spread, drift, upt, up1)
            if keep is not None:
                v = jnp.where(keep, v, 0.0)
            store(s, p, v)


def velocity_kernel(own_ref, slot_ref, recv, drift, blocks, slabs):
    me = lax.axis_index("gx")
    blocks[...] = jnp.zeros(blocks.shape, F32)
    slabs[...] = jnp.zeros(slabs.shape, F32)
    for m in range(16):
        own, low, high = jnp.int32(16), jnp.int32(16), jnp.int32(16)
        for b in range(4):
            o = own_ref[0, 4 * m + b]
            at = slot_ref[0, 4 * m + b]
            own = jnp.where(o == me, at, own)
            low = jnp.where(o == me - 1, at, low)
            high = jnp.where(o == me + 1, at, high)
        blocks[pl.ds(pl.multiple_of(16 * own, 16), 16), :] = recv[m, 0:16]
        for a in range(3):
            slabs[a, pl.ds(low, 1), :] = recv[m, 12 + a : 13 + a]
            slabs[3 + a, pl.ds(high, 1), :] = recv[m, 15 + a : 16 + a]
    group = lax.broadcasted_iota(jnp.int32, (16, 128), 1) >> 3
    masks = [(group & (1 << bit)) != 0 for bit in range(4)]

    def turned(x):
        x = pltpu.roll(x, 8, 1, stride=8, stride_axis=0)
        for bit in range(4):
            x = jnp.where(masks[bit], pltpu.roll(x, 16 - (1 << bit), 0), x)
        return pltpu.roll(x, 0, 1, stride=8, stride_axis=0)

    for a in range(3):
        for r in range(6):
            if r == 0:
                x = slabs[a, 0:16]
            elif r == 5:
                x = slabs[3 + a, 0:16]
            else:
                x = blocks[pl.ds(4 * a + r - 1, 16, stride=16), :]
            t = turned(x)
            for h in range(2):
                u = 3.0 * t[8 * h : 8 * h + 8]
                drift[2 * a, 2 * r + h] = jnp.maximum(u, 0.0)
                drift[2 * a + 1, 2 * r + h] = -jnp.minimum(u, 0.0)


NEXT, COEF, FACE_ROWS = 64, 96, 176


def tissue1_kernel(drift, conc, diff, upt, xl, xr, za, zb, ya, yb,
                   c_out, spread_out, ma, mb, pack_lo, pack_hi, coef_lo, coef_hi):
    me = lax.axis_index("gx")
    y_even, z_even = even("gy"), even("gz")
    lane = lax.broadcasted_iota(jnp.int32, (8, 128), 1)
    z_lo = jnp.where(z_even, zb[...], za[...])
    z_hi = jnp.where(z_even, za[...], zb[...])
    zero = jnp.zeros((8, 128), F32)
    packs = [zero, zero]
    coefs = [zero, zero]
    ma[...] = jnp.zeros(ma.shape, F32)
    mb[...] = jnp.zeros(mb.shape, F32)

    def field(f, own):
        def get(p):
            if p < 0:
                return xl[slab(f, 3 + p)]
            if p > 7:
                return xr[slab(f, p - 8)]
            return own(p)
        return get

    get_d = field(4, lambda p: diff[p])
    get_u = field(5, lambda p: upt[p])
    gets = [field(s, lambda p, s=s: conc[s, p]) for s in range(4)]

    def around(s, p, c):
        a, b = ya[s, p + 2 : p + 3], yb[s, p + 2 : p + 3]
        lo, hi = jnp.where(y_even, b, a), jnp.where(y_even, a, b)
        return beside(c, lo, hi, z_lo, z_hi, 12 * s + p + 2)

    def put_rows(row, low, high):
        ma[row : row + 1] = jnp.where(y_even, high, low)
        mb[row : row + 1] = jnp.where(y_even, low, high)

    def put_lanes(pair, j, value, depth):
        at = lane == j
        pair[0] = jnp.where(at, turn(value, j - depth), pair[0])
        pair[1] = jnp.where(at, turn(value, j - 127 + depth), pair[1])

    def get_coef(p):
        d = get_d(p)
        q = p + 2
        spread = [0.5 * (d + n) for n in (get_d(p - 1), get_d(p + 1)) + around(4, p, d)]
        flow = [drift[n, q] for n in range(6)]
        for n in range(6):
            spread_out[n, q] = spread[n]
        if 0 <= p < 8:
            fields = spread + [flow[2 * a] - flow[2 * a + 1] for a in range(3)] + [get_u(p)]
            for n, v in enumerate(fields):
                put_rows(COEF + 8 * n + p, v[0:1], v[7:8])
                put_lanes(coefs, 8 * n + p, v, 0)
        return spread, flow

    def store(s, p, v):
        c_out[s, p + 2] = v
        if -1 <= p < 9:
            put_rows(16 * s + p + 1, v[0:1], v[7:8])
            put_lanes(packs, 10 * s + p + 1, v, 0)
        if 0 <= p < 8:
            put_rows(NEXT + 8 * s + p, v[1:2], v[6:7])
            put_lanes(packs, 40 + 8 * s + p, v, 1)

    tissue(-2, 10, lambda s, p: gets[s](p), around, get_coef, get_u, me, store)
    pack_lo[...] = packs[0]
    pack_hi[...] = packs[1]
    coef_lo[...] = coefs[0]
    coef_hi[...] = coefs[1]


class Faces:
    def __init__(self, a, b):
        self.a, self.b, self.y_even = a, b, even("gy")

    def rows(self, side, start, count):
        a, b = self.a[start : start + count], self.b[start : start + count]
        return jnp.where(self.y_even, b, a) if side == 0 else jnp.where(self.y_even, a, b)


def corner_kernel(ya, yb, pack_lo, pack_hi, coef_lo, coef_hi, za, zb):
    lane = lax.broadcasted_iota(jnp.int32, (8, 128), 1)
    faces = Faces(ya, yb)
    corners = [jnp.zeros((8, 128), F32)] * 2
    for side in range(2):
        for s in range(4):
            v = faces.rows(side, 16 * s + 1, 8)
            at = lane == 4 * side + s
            corners[0] = jnp.where(at, turn(v, 4 * side + s), corners[0])
            corners[1] = jnp.where(at, turn(v, 4 * side + s - 127), corners[1])
    z_even = even("gz")
    low = (pack_lo[...], coef_lo[...], corners[0])
    high = (pack_hi[...], coef_hi[...], corners[1])
    for n in range(3):
        za[n] = jnp.where(z_even, high[n], low[n])
        zb[n] = jnp.where(z_even, low[n], high[n])


def tissue23_kernel(drift, spread, conc, upt, xl, xr, ya, yb, ma, mb, pack_lo, pack_hi, za, zb,
                    out, mid, y_face):
    me = lax.axis_index("gx")
    sub = lax.broadcasted_iota(jnp.int32, (8, 128), 0)
    lane = lax.broadcasted_iota(jnp.int32, (8, 128), 1)
    got, sent = Faces(ya, yb), Faces(ma, mb)
    z_even = even("gz")
    low = [jnp.where(z_even, zb[n], za[n]) for n in range(3)]
    high = [jnp.where(z_even, za[n], zb[n]) for n in range(3)]

    def flows(u):
        parts = []
        for v in u:
            parts += [jnp.maximum(v, 0.0), -jnp.minimum(v, 0.0)]
        return parts

    for side in range(2):
        coef = [got.rows(side, COEF + 8 * n, 8) for n in range(10)]
        cs = [got.rows(side, 16 * s + 1, 8) for s in range(4)]
        up1 = coef[9] * cs[1] / (HALF[1] + jnp.abs(cs[1]))
        for s in range(4):
            inner = sent.rows(side, 16 * s + 1, 8)
            outer = got.rows(side, NEXT + 8 * s, 8)
            j = 4 * side + s
            around = ((outer, inner) if side == 0 else (inner, outer)) + beside_z(cs[s], low[2], high[2], j, j)
            y_face[side, s] = advance(
                s, got.rows(side, 16 * s, 8), cs[s], got.rows(side, 16 * s + 2, 8), around,
                coef[:6], flows(coef[6:9]), coef[9], up1,
            )
    z_face = []
    for side, (pack, own) in enumerate(((low, pack_lo[...]), (high, pack_hi[...]))):
        coef = [turn(pack[1], -8 * n) for n in range(10)]
        flow = flows(coef[6:9])
        cs = [turn(pack[0], -(10 * s + 1)) for s in range(4)]
        up1 = coef[9] * cs[1] / (HALF[1] + jnp.abs(cs[1]))
        for s in range(4):
            edge = []
            for y_side in range(2):
                j = 4 * y_side + s
                column = jnp.broadcast_to(pack[2][:, j : j + 1], (8, 128))
                edge.append(jnp.sum(jnp.where(sub == lane, column, 0.0), axis=0, keepdims=True))
            ym = jnp.where(sub == 0, jnp.broadcast_to(edge[0], (8, 128)), pltpu.roll(cs[s], 1, 0))
            yp = jnp.where(sub == 7, jnp.broadcast_to(edge[1], (8, 128)), pltpu.roll(cs[s], 7, 0))
            inner, outer = turn(own, -(10 * s + 1)), turn(pack[0], -(40 + 8 * s))
            around = (ym, yp) + ((outer, inner) if side == 0 else (inner, outer))
            z_face.append(advance(
                s, turn(pack[0], -10 * s), cs[s], turn(pack[0], -(10 * s + 2)), around,
                coef[:6], flow, coef[9], up1,
            ))

    def get_u(p):
        return xl[slab(5, 3 + p)] if p < 0 else (xr[slab(5, p - 8)] if p > 7 else upt[p])

    def get_coef(p):
        return [spread[n, p + 2] for n in range(6)], [drift[n, p + 2] for n in range(6)]

    def around2(s, p, c):
        q = p + 1
        lo, hi = got.rows(0, 16 * s + q, 1), got.rows(1, 16 * s + q, 1)
        return beside(c, lo, hi, low[0], high[0], 10 * s + q)

    def store2(s, p, v):
        mid[s, p + 1] = v

    tissue(-1, 9, lambda s, p: conc[s, p + 2], around2, get_coef, get_u, me, store2)

    def around3(s, p, c):
        lo, hi = y_face[0, s, p : p + 1], y_face[1, s, p : p + 1]
        return beside(c, lo, hi, z_face[s], z_face[4 + s], p)

    def store3(s, p, v):
        out[s, p] = v

    tissue(0, 8, lambda s, p: mid[s, p + 1], around3, get_coef, get_u, me, store3)


VMEM = pltpu.VMEM


def call(kernel, smem, arrays, outs, scratch=(), space=VMEM, limit=8 << 20):
    return pl.pallas_call(
        kernel,
        in_specs=[pl.BlockSpec(memory_space=pltpu.SMEM)] * len(smem)
        + [pl.BlockSpec(memory_space=space)] * len(arrays),
        out_specs=tuple(pl.BlockSpec(memory_space=VMEM) for _ in outs),
        out_shape=tuple(jax.ShapeDtypeStruct(s, t) for s, t in outs),
        scratch_shapes=[VMEM(*x) if isinstance(x, tuple) else x for x in scratch],
        compiler_params=pltpu.CompilerParams(vmem_limit_bytes=limit),
        name=kernel.__name__,
    )(*smem, *arrays)


def hop(x, axis, step):
    n = lax.axis_size(axis)
    return lax.ppermute(x, axis, [(i, i + step) for i in range(n) if 0 <= i + step < n])


def swap(x, axis, first):
    n = lax.axis_size(axis)
    return lax.ppermute(x, axis, [(i, j) for i in range(n) for j in [i ^ 1 if first else ((i + 1) ^ 1) - 1] if 0 <= j < n])


def swaps(turn, ya, yb, za, zb):
    out = []
    for name, x, axis, first in (("za", za, "gz", True), ("zb", zb, "gz", False), ("ya", ya, "gy", True), ("yb", yb, "gy", False)):
        with jax.named_scope(f"{name}{turn}"):
            out.append(swap(x, axis, first))
    return tuple(out)


def shards(populations, viscosity, links, flags, neighbours, owners, slots, conc, diff, upt):
    i32 = jnp.int32
    tiles = lambda n: ((n, 8, 128), F32)
    tile = ((8, 128), F32)
    faces = lambda fields, rows: [((fields, rows, 128), F32)] * 2 + [tile, tile]
    pool = [((6, 48, 128), F32), ((18, 16, 128), F32)]
    state, lo, hi = call(
        first_kernel, (neighbours,), (populations, viscosity, links, flags, conc, diff, upt),
        [tiles(54), tiles(30), tiles(30)],
        [((20, 16, 128), F32), ((2, 16, 128), i32), ((19, 1, 4, 512), F32), ((1, 4, 512), F32),
         ((1, 4, 512), i32), ((1, 4, 512), i32), pltpu.SemaphoreType.DMA((16,))],
        space=pltpu.HBM, limit=67043328 - (420 << 10),
    )
    xl, xr = hop(hi, "gx", 1), hop(lo, "gx", -1)
    post, unit, *rim = call(
        second_kernel, (neighbours,), (state, xl, xr, conc, diff),
        [tiles(38), tiles(12)] + faces(5, 16), pool,
    )
    rim = swaps(0, *rim)
    for _ in range(FLOW_STEPS - 2):
        left, right = hop(unit, "gx", 1), hop(unit, "gx", -1)
        post, unit = call(
            step_kernel, (neighbours,), (state, post, unit, left, right), [tiles(38), tiles(12)], pool
        )
    left, right = hop(unit, "gx", 1), hop(unit, "gx", -1)
    weighted, send = call(
        last_kernel, (neighbours, owners), (state, post, unit, left, right),
        [((19, 1, 4, 512), F32), ((16, 24, 128), F32)],
        pool + [((19, 16, 128), F32), ((3, 16, 128), F32)],
    )
    with jax.named_scope("spread"):
        recv = lax.all_to_all(send, "gx", 0, 0)
    with jax.named_scope("drift"):
        (drift,) = call(
            velocity_kernel, (owners, slots), (recv,), [((6, 12, 8, 128), F32)],
            [((17 * 16, 128), F32), ((6, 24, 128), F32)],
        )
    face = ((FACE_ROWS, 128), F32)
    c1, spread, ma, mb, pack_lo, pack_hi, coef_lo, coef_hi = call(
        tissue1_kernel, (), (drift, conc, diff, upt, xl, xr) + rim,
        [((4, 12, 8, 128), F32), ((6, 12, 8, 128), F32), face, face] + [tile] * 4,
    )
    ya, yb = swap(ma, "gy", True), swap(mb, "gy", False)
    za, zb = call(
        corner_kernel, (), (ya, yb, pack_lo, pack_hi, coef_lo, coef_hi), [tiles(3), tiles(3)]
    )
    za, zb = swap(za, "gz", True), swap(zb, "gz", False)
    (out,) = call(
        tissue23_kernel, (),
        (drift, spread, c1, upt, xl, xr, ya, yb, ma, mb, pack_lo, pack_hi, za, zb),
        [((4, 8, 8, 128), F32)], [((4, 10, 8, 128), F32), ((2, 4, 8, 128), F32)],
    )
    return weighted, out


def solution(mesh):
    site = P(("gy", "gz"), "gx", None)
    brick = P("gx", "gy", "gz")
    return jax.shard_map(
        shards,
        mesh=mesh,
        in_specs=(
            P(None, ("gy", "gz"), "gx", None), site, site, site, site,
            P(("gy", "gz"), None), P(("gy", "gz"), None),
            P(None, "gx", "gy", "gz"), brick, brick,
        ),
        out_specs=(P(None, ("gy", "gz"), "gx", None), P(None, "gx", "gy", "gz")),
        check_vma=False,
    )
```

```python
import jax
import jax.numpy as jnp
import numpy as np
from jax import lax
from jax.experimental import pallas as pl
from jax.experimental.pallas import tpu as pltpu
from jax.sharding import PartitionSpec as P


FLOW_STEPS = 4
DIRS = (
    (0, 0, 0),
    (1, 0, 0), (-1, 0, 0), (0, 1, 0), (0, -1, 0), (0, 0, 1), (0, 0, -1),
    (1, 1, 0), (-1, -1, 0), (1, -1, 0), (-1, 1, 0),
    (1, 0, 1), (-1, 0, -1), (1, 0, -1), (-1, 0, 1),
    (0, 1, 1), (0, -1, -1), (0, 1, -1), (0, -1, 1),
)
WEIGHT = (1.0 / 3.0,) + (1.0 / 18.0,) * 6 + (1.0 / 36.0,) * 12
OPP = tuple(DIRS.index(tuple(-v for v in c)) for c in DIRS)
GAIN = (1.0, 0.6, 0.7, 0.35)
HALF = (0.3, 0.5, 0.8, 0.2)
STRIDE = (64, 8, 1)
SITE = np.arange(512)
COORD = np.stack([SITE // 64, SITE // 8 % 8, SITE % 8], axis=1)
UNITS = tuple((a, s) for a in range(3) for s in (1, -1))
UNIT_POPS = tuple(tuple(i for i in range(1, 19) if DIRS[i][a] == s) for a, s in UNITS)
UNIT_SLOT = tuple(
    ((7, 5, 3, 1, 6) if a == 0 else (7, 6, 5, 4, 3))
    if s == 1
    else ((0, 2, 4, 6, 1) if a == 0 else (0, 1, 2, 3, 4))
    for a, s in UNITS
)
F32 = jnp.float32
GRID = (2, 8, 128)


def unit_of(a, s):
    return 2 * a + (0 if s == 1 else 1)


def dir_index(vec):
    return DIRS.index(tuple(vec)) - 1


def edge_unit(i):
    axes = [a for a in range(3) if DIRS[i][a]]
    return axes[1], axes[0]


class Sites:
    def __init__(self):
        sub = lax.broadcasted_iota(jnp.int32, GRID, 1)
        self.lane = lax.broadcasted_iota(jnp.int32, GRID, 2)
        self.sub = sub
        self.coord = (
            (sub & 3) * 2 + (self.lane >> 6),
            (self.lane >> 3) & 7,
            self.lane & 7,
        )
        self.cache = {}

    def plane(self, a, value):
        key = (a, value)
        if key not in self.cache:
            self.cache[key] = self.coord[a] == value
        return self.cache[key]

    def roll(self, v, n, dest):
        low = n % 128
        rows = (n - low) // 128
        lanes = SITE[dest] % 128

        def shift(x, k):
            return pltpu.roll(x, k % 8, 1) if k % 8 else x

        r = pltpu.roll(v, low, 2) if low else v
        same, carried = (lanes >= low).any(), (lanes < low).any()
        if same and carried:
            return jnp.where(self.lane >= low, shift(r, rows), shift(r, rows + 1))
        return shift(r, rows if same else rows + 1)


def moments(f):
    j = []
    for a in range(3):
        t = None
        for i in range(1, 19):
            if DIRS[i][a] == 0:
                continue
            if t is None:
                t = f[i] if DIRS[i][a] == 1 else -f[i]
            else:
                t = t + f[i] if DIRS[i][a] == 1 else t - f[i]
        j.append(t)
    return j


def equilibrium(r, j):
    base = r - 1.5 * (j[0] * j[0] + j[1] * j[1] + j[2] * j[2])
    out = [base * WEIGHT[0]] + [None] * 18
    for i in range(1, 19, 2):
        c = DIRS[i]
        p = None
        for a in range(3):
            if c[a]:
                t = j[a] if c[a] == 1 else -j[a]
                p = t if p is None else p + t
        even = base + 4.5 * (p * p)
        odd = 3.0 * p
        out[i] = WEIGHT[i] * (even + odd)
        out[i + 1] = WEIGHT[i] * (even - odd)
    return out


CODE = 38


def collide_pack(sites, f, relax, post_ref, unit_ref, base=0):
    r = f[0]
    for i in range(1, 19):
        r = r + f[i]
    feq = equilibrium(r, moments(f))
    post = [f[i] - relax * (f[i] - feq[i]) for i in range(19)]
    for i in range(19):
        post_ref[2 * i : 2 * i + 2] = post[i]
    for u, (a, s) in enumerate(UNITS):
        src = 7 if s == 1 else 0
        acc = post[UNIT_POPS[u][0]]
        for i, slot in list(zip(UNIT_POPS[u], UNIT_SLOT[u]))[1:]:
            moved = sites.roll(post[i], (slot - src) * STRIDE[a], COORD[:, a] == slot)
            acc = jnp.where(sites.plane(a, slot), moved, acc)
        unit_ref[base + 2 * u : base + 2 * u + 2] = acc


def stream(sites, me, nbr_ref, post_ref, unit_ref, left_ref, right_ref, code_ref, pool, got, base=0):
    for u in range(6):
        pool[u, 0:16] = left_ref[2 * u : 2 * u + 2].reshape(16, 128)
        pool[u, 16:32] = unit_ref[base + 2 * u : base + 2 * u + 2].reshape(16, 128)
        pool[u, 32:48] = right_ref[2 * u : 2 * u + 2].reshape(16, 128)
    first = (me - 1) * 4
    for k in range(18):
        d = DIRS[k + 1]
        i = OPP[k + 1]
        axes = [a for a in range(3) if d[a]]
        a = axes[0] if len(axes) == 1 else edge_unit(i)[0]
        u = unit_of(a, -d[a])
        for b in range(4):
            n = jnp.clip(nbr_ref[0, b, k] - first, 0, 11)
            got[k, 4 * b : 4 * b + 4] = pool[u, pl.ds(pl.multiple_of(4 * n, 4), 4), :]
    eff = code_ref[CODE + 2 : CODE + 4].astype(jnp.int32)
    f = [post_ref[0:2]]
    for i in range(1, 19):
        c = DIRS[i]
        axes = [a for a in range(3) if c[a]]
        dest = {a: (0 if c[a] == 1 else 7) for a in axes}
        at = {a: COORD[:, a] == dest[a] for a in axes}
        shift = sum(c[a] * STRIDE[a] for a in range(3))
        pulled = sites.roll(post_ref[2 * i : 2 * i + 2], shift, ~np.any([at[a] for a in axes], axis=0))
        for a in axes:
            u = unit_of(a, c[a])
            slot = UNIT_SLOT[u][UNIT_POPS[u].index(i)]
            face = [0, 0, 0]
            face[a] = -c[a]
            n = (dest[a] - slot) * STRIDE[a] + shift - c[a] * STRIDE[a]
            where = at[a].copy()
            for o in axes:
                if o != a:
                    where &= ~at[o]
            v = sites.roll(got[dir_index(face)].reshape(GRID), n, where)
            pulled = jnp.where(sites.plane(a, dest[a]), v, pulled)
        if len(axes) == 2:
            a, o = edge_unit(i)
            u = unit_of(a, c[a])
            slot = UNIT_SLOT[u][UNIT_POPS[u].index(i)]
            n = (dest[a] - slot) * STRIDE[a] + (dest[o] - (7 - dest[o])) * STRIDE[o]
            v = sites.roll(got[dir_index([-t for t in c])].reshape(GRID), n, at[a] & at[o])
            both = sites.plane(a, dest[a]) & sites.plane(o, dest[o])
            pulled = jnp.where(both, v, pulled)
        o = OPP[i]
        f.append(jnp.where((eff & (1 << (i - 1))) != 0, pulled, post_ref[2 * o : 2 * o + 2]))
    flag = eff >> 18
    feq = equilibrium(jnp.where(flag == 1, 1.03, 0.97).astype(F32), moments(f))
    edge = flag > 0
    return [jnp.where(edge, feq[i], f[i]) for i in range(19)]


def to_rows(dst, value):
    for r in range(4):
        dst[pl.ds(r, 4, stride=4), :] = value[:, 128 * r : 128 * r + 128]


def slab(field, plane):
    return 12 + 3 * field + plane


def first_kernel(nbr_ref, pop_hbm, visc_hbm, link_hbm, flag_hbm, conc_hbm, diff_hbm, upt_hbm,
                 state, lo, hi,
                 rows, irows, pop_ref, visc_ref, link_ref, flag_in, sem):
    pairs = [(pop_hbm, pop_ref), (visc_hbm, visc_ref), (link_hbm, link_ref), (flag_hbm, flag_in)]
    for out, base in ((lo, 0), (hi, 5)):
        fields = [conc_hbm.at[s] for s in range(4)] + [diff_hbm, upt_hbm]
        for n, field in enumerate(fields):
            pairs.append((field.at[base : base + 3], out.at[slab(n, 0) : slab(n, 3)]))
    copies = [pltpu.make_async_copy(src, dst, sem.at[n]) for n, (src, dst) in enumerate(pairs)]
    for copy in copies:
        copy.start()
    for copy in copies:
        copy.wait()
    sites = Sites()
    f = []
    for i in range(19):
        to_rows(rows.at[i], pop_ref[i, 0])
    to_rows(rows.at[19], visc_ref[0])
    to_rows(irows.at[0], link_ref[0])
    to_rows(irows.at[1], flag_in[0])
    f = [rows[i].reshape(GRID) * np.float32(WEIGHT[i]) for i in range(19)]
    relax = 1.0 / (3.0 * rows[19].reshape(GRID) + 0.5)
    state[38:40] = relax
    group = lax.broadcasted_iota(jnp.int32, GRID, 0) * 2 + (sites.sub >> 2)
    closed = jnp.zeros(GRID, jnp.int32)
    zero = jnp.zeros(GRID, jnp.int32)
    for k in range(18):
        d = DIRS[k + 1]
        axes = [a for a in range(3) if d[a]]
        if len(axes) == 1:
            a = axes[0]
            s = -d[a]
            bits = jnp.full(GRID, 1 << (OPP[k + 1] - 1), jnp.int32)
            for i in UNIT_POPS[unit_of(a, s)]:
                others = [o for o in range(3) if o != a and DIRS[i][o]]
                if others:
                    o = others[0]
                    off = sites.plane(o, 0 if DIRS[i][o] == 1 else 7)
                    bits = bits | jnp.where(off, 0, 1 << (i - 1))
            bits = jnp.where(sites.plane(a, 0 if s == 1 else 7), bits, 0)
        else:
            i = OPP[k + 1]
            c = DIRS[i]
            a, o = axes
            at = sites.plane(a, 0 if c[a] == 1 else 7) & sites.plane(o, 0 if c[o] == 1 else 7)
            bits = jnp.where(at, 1 << (i - 1), 0)
        gone = [(nbr_ref[0, b, k] < 0).astype(jnp.int32) for b in range(4)]
        miss = jnp.where(
            group < 2,
            jnp.where(group == 0, gone[0], gone[1]),
            jnp.where(group == 2, gone[2], gone[3]),
        )
        closed = closed | jnp.where(miss != 0, bits, zero)
    code = (irows[0].reshape(GRID) & ~closed & ((1 << 18) - 1)) + (irows[1].reshape(GRID) << 18)
    state[40:42] = code.astype(F32)
    collide_pack(sites, f, relax, state, state, CODE + 4)
    lo[0:12] = state[42:54]
    hi[0:12] = state[42:54]


def step_kernel(nbr_ref, state, post_in, unit_in, left_ref, right_ref, post_ref, unit_ref, pool, got):
    sites = Sites()
    me = lax.axis_index("gx")
    f = stream(sites, me, nbr_ref, post_in, unit_in, left_ref, right_ref, state, pool, got)
    collide_pack(sites, f, state[CODE : CODE + 2], post_ref, unit_ref)


def second_kernel(nbr_ref, state, left_ref, right_ref, conc, diff,
                  post_ref, unit_ref, ya, yb, za, zb, pool, got):
    sites = Sites()
    me = lax.axis_index("gx")
    f = stream(sites, me, nbr_ref, state, state, left_ref, right_ref, state, pool, got, CODE + 4)
    collide_pack(sites, f, state[CODE : CODE + 2], post_ref, unit_ref)
    first_rims(conc, diff, left_ref, right_ref, ya, yb, za, zb)


def last_kernel(nbr_ref, own_ref, slot_ref, state, post_in, unit_in, left_ref, right_ref, f_ref, send_ref, pool, got, jrows):
    sites = Sites()
    me = lax.axis_index("gx")
    f = stream(sites, me, nbr_ref, post_in, unit_in, left_ref, right_ref, state, pool, got)
    for i in range(19):
        f_ref[i] = f[i].reshape(16, 128)
    j = moments(f)
    for a in range(3):
        v = j[a]
        for bit in (8, 16, 32, 64):
            up = pltpu.roll(v, bit, 2)
            down = up if bit == 64 else pltpu.roll(v, 128 - bit, 2)
            v = jnp.where((sites.lane & bit) != 0, up, down)
        jrows[a] = v.reshape(16, 128)
    send_ref[...] = jnp.zeros(send_ref.shape, F32)
    for b in range(4):
        o = own_ref[0, 4 * me + b]
        for a in range(3):
            for r in range(4):
                send_ref[o, 2 * a + r // 2, r % 2 : r % 2 + 1] = jrows[a, 4 * b + r : 4 * b + r + 1]

        @pl.when(o < 15)
        def _():
            for a in range(3):
                k = 12 + a
                send_ref[o + 1, k // 2, k % 2 : k % 2 + 1] = jrows[a, 4 * b + 3 : 4 * b + 4]

        @pl.when(o > 0)
        def _():
            for a in range(3):
                k = 15 + a
                send_ref[o - 1, k // 2, k % 2 : k % 2 + 1] = jrows[a, 4 * b : 4 * b + 1]


def weighted_kernel(f_ref, out_ref):
    for i in range(19):
        for r in range(4):
            rows = f_ref[i, pl.ds(r, 4, stride=4), :]
            out_ref[i, 0, :, 128 * r : 128 * r + 128] = rows * np.float32(1.0 / WEIGHT[i])


def even(axis):
    return lax.rem(lax.axis_index(axis), 2) == 0


class Rims:
    def __init__(self, lane, ya, yb):
        self.lane, self.ya, self.yb = lane, ya, yb
        self.lo = jnp.zeros((8, 128), F32)
        self.hi = jnp.zeros((8, 128), F32)
        self.y_even = even("gy")

    def put(self, value, j, s, row):
        self.ya[s, row : row + 1] = jnp.where(self.y_even, value[7:8], value[0:1])
        self.yb[s, row : row + 1] = jnp.where(self.y_even, value[0:1], value[7:8])
        at = self.lane == j
        self.lo = jnp.where(at, pltpu.roll(value, j, 1) if j else value, self.lo)
        self.hi = jnp.where(at, pltpu.roll(value, (j + 1) % 128, 1), self.hi)

    def finish(self, za, zb):
        z_even = even("gz")
        za[...] = jnp.where(z_even, self.hi, self.lo)
        zb[...] = jnp.where(z_even, self.lo, self.hi)


def first_rims(conc, diff, xl, xr, ya, yb, za, zb):
    lane = lax.broadcasted_iota(jnp.int32, (8, 128), 1)
    rims = Rims(lane, ya, yb)
    for fld in range(5):
        for p in range(12):
            q = p - 2
            if q < 0:
                v = xl[slab(fld, 3 + q)]
            elif q > 7:
                v = xr[slab(fld, q - 8)]
            else:
                v = conc[fld, q] if fld < 4 else diff[q]
            rims.put(v, fld * 12 + p, fld, p)
    rims.finish(za, zb)


def beside(v, lo, hi, z_lo, z_hi, j):
    sub = lax.broadcasted_iota(jnp.int32, (8, 128), 0)
    lane = lax.broadcasted_iota(jnp.int32, (8, 128), 1)
    ym = jnp.where(sub == 0, jnp.broadcast_to(lo, (8, 128)), pltpu.roll(v, 1, 0))
    yp = jnp.where(sub == 7, jnp.broadcast_to(hi, (8, 128)), pltpu.roll(v, 7, 0))
    return (ym, yp) + beside_z(v, z_lo, z_hi, j, j)


def beside_z(v, z_lo, z_hi, j_lo, j_hi):
    lane = lax.broadcasted_iota(jnp.int32, (8, 128), 1)
    zm = jnp.where(lane == 0, turn(z_lo, -j_lo), pltpu.roll(v, 1, 1))
    zp = jnp.where(lane == 127, turn(z_hi, 127 - j_hi), pltpu.roll(v, 127, 1))
    return zm, zp


def turn(v, n):
    return pltpu.roll(v, n % 128, 1) if n % 128 else v


def advance(s, cm, c, cp, around, spread, drift, upt, up1):
    k = GAIN[s]
    acc = c
    for v, g, d in zip((cm, cp) + tuple(around), spread, drift):
        w = d + (g if k == 1.0 else k * g)
        acc = acc + w * (v - c)
    if s == 2:
        return acc + 2.0 * up1
    return acc - upt * c / (HALF[s] + jnp.abs(c))


def tissue(lo, hi, get_c, around, get_coef, get_upt, me, store):
    for p in range(lo, hi):
        spread, drift = get_coef(p)
        upt = get_upt(p)
        keep = me > 0 if p < 0 else (me < 15 if p > 7 else None)
        c1 = get_c(1, p)
        up1 = upt * c1 / (HALF[1] + jnp.abs(c1))
        for s in range(4):
            c = get_c(s, p)
            v = advance(s, get_c(s, p - 1), c, get_c(s, p + 1), around(s, p, c), spread, drift, upt, up1)
            if keep is not None:
                v = jnp.where(keep, v, 0.0)
            store(s, p, v)


def place_velocity(own_ref, slot_ref, recv, drift, blocks, slabs):
    me = lax.axis_index("gx")
    blocks[...] = jnp.zeros(blocks.shape, F32)
    slabs[...] = jnp.zeros(slabs.shape, F32)
    for m in range(16):
        own, low, high = jnp.int32(16), jnp.int32(16), jnp.int32(16)
        for b in range(4):
            o = own_ref[0, 4 * m + b]
            at = slot_ref[0, 4 * m + b]
            own = jnp.where(o == me, at, own)
            low = jnp.where(o == me - 1, at, low)
            high = jnp.where(o == me + 1, at, high)
        for k in range(18):
            row = recv[m, k // 2, k % 2 : k % 2 + 1]
            if k < 12:
                blocks[pl.ds(16 * own + k, 1), :] = row
            else:
                slabs[k - 12, pl.ds(low if k < 15 else high, 1), :] = row
    group = lax.broadcasted_iota(jnp.int32, (16, 128), 1) >> 3
    masks = [(group & (1 << bit)) != 0 for bit in range(4)]

    def turned(x):
        x = pltpu.roll(x, 8, 1, stride=8, stride_axis=0)
        for bit in range(4):
            x = jnp.where(masks[bit], pltpu.roll(x, 16 - (1 << bit), 0), x)
        return pltpu.roll(x, 0, 1, stride=8, stride_axis=0)

    for a in range(3):
        for r in range(6):
            if r == 0:
                x = slabs[a, 0:16]
            elif r == 5:
                x = slabs[3 + a, 0:16]
            else:
                x = blocks[pl.ds(4 * a + r - 1, 16, stride=16), :]
            t = turned(x)
            for h in range(2):
                u = 3.0 * t[8 * h : 8 * h + 8]
                drift[2 * a, 2 * r + h] = jnp.maximum(u, 0.0)
                drift[2 * a + 1, 2 * r + h] = -jnp.minimum(u, 0.0)


NEXT, COEF, FACE_ROWS = 64, 96, 176


def brick_field(xl, xr, f, own):
    def get(p):
        if p < 0:
            return xl[slab(f, 3 + p)]
        if p > 7:
            return xr[slab(f, p - 8)]
        return own(p)

    return get


def first_around(za, zb, ya, yb):
    y_even, z_even = even("gy"), even("gz")
    z_lo = jnp.where(z_even, zb[...], za[...])
    z_hi = jnp.where(z_even, za[...], zb[...])

    def around(s, p, c):
        a, b = ya[s, p + 2 : p + 3], yb[s, p + 2 : p + 3]
        lo, hi = jnp.where(y_even, b, a), jnp.where(y_even, a, b)
        return beside(c, lo, hi, z_lo, z_hi, 12 * s + p + 2)

    return around


def put_rows(ma, mb, y_even, row, low, high):
    ma[row : row + 1] = jnp.where(y_even, high, low)
    mb[row : row + 1] = jnp.where(y_even, low, high)


def put_lanes(pair, j, value, depth):
    at = lax.broadcasted_iota(jnp.int32, (8, 128), 1) == j
    pair[0] = jnp.where(at, turn(value, j - depth), pair[0])
    pair[1] = jnp.where(at, turn(value, j - 127 + depth), pair[1])


def spread_kernel(conc, diff, upt, xl, xr, za, zb, ya, yb, part, spread_out, ca, cb, coef_lo, coef_hi):
    y_even = even("gy")
    around = first_around(za, zb, ya, yb)
    coefs = [jnp.zeros((8, 128), F32)] * 2
    get_d = brick_field(xl, xr, 4, lambda p: diff[p])
    get_u = brick_field(xl, xr, 5, lambda p: upt[p])
    gets = [brick_field(xl, xr, s, lambda p, s=s: conc[s, p]) for s in range(4)]
    for p in range(-2, 10):
        d, u = get_d(p), get_u(p)
        spread = [0.5 * (d + n) for n in (get_d(p - 1), get_d(p + 1)) + around(4, p, d)]
        for n in range(6):
            spread_out[n, p + 2] = spread[n]
        if 0 <= p < 8:
            for n, v in enumerate(spread + [u]):
                put_rows(ca, cb, y_even, 8 * n + p, v[0:1], v[7:8])
                put_lanes(coefs, 8 * n + p, v, 0)
        c1 = gets[1](p)
        up1 = u * c1 / (HALF[1] + jnp.abs(c1))
        for s in range(4):
            c = gets[s](p)
            total = None
            for g, v in zip(spread, (gets[s](p - 1), gets[s](p + 1)) + around(s, p, c)):
                t = g * (v - c)
                total = t if total is None else total + t
            v = c + GAIN[s] * total
            part[s, p + 2] = v + 2.0 * up1 if s == 2 else v - u * c / (HALF[s] + jnp.abs(c))
    coef_lo[...] = coefs[0]
    coef_hi[...] = coefs[1]


def drift_kernel(own_ref, slot_ref, recv, part, conc, xl, xr, za, zb, ya, yb, ca, cb, coef_lo_in, coef_hi_in,
                 drift, c_out, ma, mb, pack_lo, pack_hi, coef_lo, coef_hi, blocks, slabs):
    me = lax.axis_index("gx")
    y_even = even("gy")
    place_velocity(own_ref, slot_ref, recv, drift, blocks, slabs)
    around = first_around(za, zb, ya, yb)
    gets = [brick_field(xl, xr, s, lambda p, s=s: conc[s, p]) for s in range(4)]
    packs = [jnp.zeros((8, 128), F32)] * 2
    coefs = [coef_lo_in[...], coef_hi_in[...]]
    ma[0:COEF] = jnp.zeros((COEF, 128), F32)
    mb[0:COEF] = jnp.zeros((COEF, 128), F32)
    ma[COEF : COEF + 56] = ca[...]
    mb[COEF : COEF + 56] = cb[...]
    for p in range(-2, 10):
        flow = [drift[n, p + 2] for n in range(6)]
        if 0 <= p < 8:
            for a in range(3):
                v = flow[2 * a] - flow[2 * a + 1]
                put_rows(ma, mb, y_even, COEF + 8 * (7 + a) + p, v[0:1], v[7:8])
                put_lanes(coefs, 8 * (7 + a) + p, v, 0)
        keep = me > 0 if p < 0 else (me < 15 if p > 7 else None)
        for s in range(4):
            c = gets[s](p)
            v = part[s, p + 2]
            for d, n in zip(flow, (gets[s](p - 1), gets[s](p + 1)) + around(s, p, c)):
                v = v + d * (n - c)
            if keep is not None:
                v = jnp.where(keep, v, 0.0)
            c_out[s, p + 2] = v
            if -1 <= p < 9:
                put_rows(ma, mb, y_even, 16 * s + p + 1, v[0:1], v[7:8])
                put_lanes(packs, 10 * s + p + 1, v, 0)
            if 0 <= p < 8:
                put_rows(ma, mb, y_even, NEXT + 8 * s + p, v[1:2], v[6:7])
                put_lanes(packs, 40 + 8 * s + p, v, 1)
    pack_lo[...] = packs[0]
    pack_hi[...] = packs[1]
    coef_lo[...] = coefs[0]
    coef_hi[...] = coefs[1]


class Faces:
    def __init__(self, a, b):
        self.a, self.b, self.y_even = a, b, even("gy")

    def rows(self, side, start, count):
        a, b = self.a[start : start + count], self.b[start : start + count]
        return jnp.where(self.y_even, b, a) if side == 0 else jnp.where(self.y_even, a, b)


def corner_kernel(ya, yb, pack_lo, pack_hi, coef_lo, coef_hi, za, zb):
    lane = lax.broadcasted_iota(jnp.int32, (8, 128), 1)
    faces = Faces(ya, yb)
    corners = [jnp.zeros((8, 128), F32)] * 2
    for side in range(2):
        for s in range(4):
            v = faces.rows(side, 16 * s + 1, 8)
            at = lane == 4 * side + s
            corners[0] = jnp.where(at, turn(v, 4 * side + s), corners[0])
            corners[1] = jnp.where(at, turn(v, 4 * side + s - 127), corners[1])
    z_even = even("gz")
    low = (pack_lo[...], coef_lo[...], corners[0])
    high = (pack_hi[...], coef_hi[...], corners[1])
    for n in range(3):
        za[n] = jnp.where(z_even, high[n], low[n])
        zb[n] = jnp.where(z_even, low[n], high[n])


def tissue23_kernel(drift, spread, conc, upt, xl, xr, ya, yb, ma, mb, pack_lo, pack_hi, za, zb,
                    out, mid, y_face):
    me = lax.axis_index("gx")
    sub = lax.broadcasted_iota(jnp.int32, (8, 128), 0)
    lane = lax.broadcasted_iota(jnp.int32, (8, 128), 1)
    got, sent = Faces(ya, yb), Faces(ma, mb)
    z_even = even("gz")
    low = [jnp.where(z_even, zb[n], za[n]) for n in range(3)]
    high = [jnp.where(z_even, za[n], zb[n]) for n in range(3)]

    def flows(u):
        parts = []
        for v in u:
            parts += [jnp.maximum(v, 0.0), -jnp.minimum(v, 0.0)]
        return parts

    for side in range(2):
        coef = [got.rows(side, COEF + 8 * n, 8) for n in range(10)]
        cs = [got.rows(side, 16 * s + 1, 8) for s in range(4)]
        up1 = coef[6] * cs[1] / (HALF[1] + jnp.abs(cs[1]))
        for s in range(4):
            inner = sent.rows(side, 16 * s + 1, 8)
            outer = got.rows(side, NEXT + 8 * s, 8)
            j = 4 * side + s
            around = ((outer, inner) if side == 0 else (inner, outer)) + beside_z(cs[s], low[2], high[2], j, j)
            y_face[side, s] = advance(
                s, got.rows(side, 16 * s, 8), cs[s], got.rows(side, 16 * s + 2, 8), around,
                coef[:6], flows(coef[7:10]), coef[6], up1,
            )
    z_face = []
    for side, (pack, own) in enumerate(((low, pack_lo[...]), (high, pack_hi[...]))):
        coef = [turn(pack[1], -8 * n) for n in range(10)]
        flow = flows(coef[7:10])
        cs = [turn(pack[0], -(10 * s + 1)) for s in range(4)]
        up1 = coef[6] * cs[1] / (HALF[1] + jnp.abs(cs[1]))
        for s in range(4):
            edge = []
            for y_side in range(2):
                j = 4 * y_side + s
                column = jnp.broadcast_to(pack[2][:, j : j + 1], (8, 128))
                edge.append(jnp.sum(jnp.where(sub == lane, column, 0.0), axis=0, keepdims=True))
            ym = jnp.where(sub == 0, jnp.broadcast_to(edge[0], (8, 128)), pltpu.roll(cs[s], 1, 0))
            yp = jnp.where(sub == 7, jnp.broadcast_to(edge[1], (8, 128)), pltpu.roll(cs[s], 7, 0))
            inner, outer = turn(own, -(10 * s + 1)), turn(pack[0], -(40 + 8 * s))
            around = (ym, yp) + ((outer, inner) if side == 0 else (inner, outer))
            z_face.append(advance(
                s, turn(pack[0], -10 * s), cs[s], turn(pack[0], -(10 * s + 2)), around,
                coef[:6], flow, coef[6], up1,
            ))

    def get_u(p):
        return xl[slab(5, 3 + p)] if p < 0 else (xr[slab(5, p - 8)] if p > 7 else upt[p])

    def get_coef(p):
        return [spread[n, p + 2] for n in range(6)], [drift[n, p + 2] for n in range(6)]

    def around2(s, p, c):
        q = p + 1
        lo, hi = got.rows(0, 16 * s + q, 1), got.rows(1, 16 * s + q, 1)
        return beside(c, lo, hi, low[0], high[0], 10 * s + q)

    def store2(s, p, v):
        mid[s, p + 1] = v

    tissue(-1, 9, lambda s, p: conc[s, p + 2], around2, get_coef, get_u, me, store2)

    def around3(s, p, c):
        lo, hi = y_face[0, s, p : p + 1], y_face[1, s, p : p + 1]
        return beside(c, lo, hi, z_face[s], z_face[4 + s], p)

    def store3(s, p, v):
        out[s, p] = v

    tissue(0, 8, lambda s, p: mid[s, p + 1], around3, get_coef, get_u, me, store3)


VMEM = pltpu.VMEM


def call(kernel, smem, arrays, outs, scratch=(), space=VMEM, limit=8 << 20):
    return pl.pallas_call(
        kernel,
        in_specs=[pl.BlockSpec(memory_space=pltpu.SMEM)] * len(smem)
        + [pl.BlockSpec(memory_space=space)] * len(arrays),
        out_specs=tuple(pl.BlockSpec(memory_space=VMEM) for _ in outs),
        out_shape=tuple(jax.ShapeDtypeStruct(s, t) for s, t in outs),
        scratch_shapes=[VMEM(*x) if isinstance(x, tuple) else x for x in scratch],
        compiler_params=pltpu.CompilerParams(vmem_limit_bytes=limit),
    )(*smem, *arrays)


def hop(x, axis, step):
    n = lax.axis_size(axis)
    return lax.ppermute(x, axis, [(i, i + step) for i in range(n) if 0 <= i + step < n])


def swap(x, axis, first):
    n = lax.axis_size(axis)
    return lax.ppermute(x, axis, [(i, j) for i in range(n) for j in [i ^ 1 if first else ((i + 1) ^ 1) - 1] if 0 <= j < n])


def swaps(ya, yb, za, zb):
    out = []
    for x, axis, first in ((za, "gz", True), (zb, "gz", False), (ya, "gy", True), (yb, "gy", False)):
        out.append(swap(x, axis, first))
    return tuple(out)


def program(populations, viscosity, links, flags, neighbours, owners, slots, conc, diff, upt):
    i32 = jnp.int32
    tiles = lambda n: ((n, 8, 128), F32)
    tile = ((8, 128), F32)
    faces = lambda fields, rows: [((fields, rows, 128), F32)] * 2 + [tile, tile]
    pool = [((6, 48, 128), F32), ((18, 16, 128), F32)]
    state, lo, hi = call(
        first_kernel, (neighbours,), (populations, viscosity, links, flags, conc, diff, upt),
        [tiles(54), tiles(30), tiles(30)],
        [((20, 16, 128), F32), ((2, 16, 128), i32), ((19, 1, 4, 512), F32), ((1, 4, 512), F32),
         ((1, 4, 512), i32), ((1, 4, 512), i32), pltpu.SemaphoreType.DMA((16,))],
        space=pltpu.HBM, limit=67043328 - (420 << 10),
    )
    xl, xr = hop(hi, "gx", 1), hop(lo, "gx", -1)
    post, unit, *rim = call(
        second_kernel, (neighbours,), (state, xl, xr, conc, diff),
        [tiles(38), tiles(12)] + faces(5, 16), pool,
    )
    rim = swaps(*rim)
    for _ in range(FLOW_STEPS - 2):
        left, right = hop(unit, "gx", 1), hop(unit, "gx", -1)
        post, unit = call(
            step_kernel, (neighbours,), (state, post, unit, left, right), [tiles(38), tiles(12)], pool
        )
    left, right = hop(unit, "gx", 1), hop(unit, "gx", -1)
    last, send = call(
        last_kernel, (neighbours, owners, slots), (state, post, unit, left, right),
        [((19, 16, 128), F32), ((16, 9, 2, 128), F32)], pool + [((3, 16, 128), F32)],
    )
    recv = lax.all_to_all(send, "gx", 0, 0)
    (weighted,) = call(weighted_kernel, (), (last,), [((19, 1, 4, 512), F32)])
    face = ((FACE_ROWS, 128), F32)
    twelve = lambda n: ((n, 12, 8, 128), F32)
    part, spread, ca, cb, coef_lo, coef_hi = call(
        spread_kernel, (), (conc, diff, upt, xl, xr) + rim,
        [twelve(4), twelve(6), ((56, 128), F32), ((56, 128), F32), tile, tile],
    )
    drift, c1, ma, mb, pack_lo, pack_hi, coef_lo, coef_hi = call(
        drift_kernel, (owners, slots), (recv, part, conc, xl, xr) + rim + (ca, cb, coef_lo, coef_hi),
        [twelve(6), twelve(4), face, face] + [tile] * 4,
        [((17 * 16, 128), F32), ((6, 24, 128), F32)],
    )
    ya = swap(ma, "gy", True)
    yb = swap(mb, "gy", False)
    za, zb = call(
        corner_kernel, (), (ya, yb, pack_lo, pack_hi, coef_lo, coef_hi), [tiles(3), tiles(3)]
    )
    za, zb = swap(za, "gz", True), swap(zb, "gz", False)
    (out,) = call(
        tissue23_kernel, (),
        (drift, spread, c1, upt, xl, xr, ya, yb, ma, mb, pack_lo, pack_hi, za, zb),
        [((4, 8, 8, 128), F32)], [((4, 10, 8, 128), F32), ((2, 4, 8, 128), F32)],
    )
    return weighted, out


def solution(mesh):
    site = P(("gy", "gz"), "gx", None)
    brick = P("gx", "gy", "gz")
    return jax.shard_map(
        program,
        mesh=mesh,
        in_specs=(
            P(None, ("gy", "gz"), "gx", None), site, site, site, site,
            P(("gy", "gz"), None), P(("gy", "gz"), None),
            P(None, "gx", "gy", "gz"), brick, brick,
        ),
        out_specs=(P(None, ("gy", "gz"), "gx", None), P(None, "gx", "gy", "gz")),
        check_vma=False,
    )
```

```python
import jax
import jax.numpy as jnp
import numpy as np
from jax import lax
from jax.experimental import pallas as pl
from jax.experimental.pallas import tpu as pltpu
from jax.sharding import PartitionSpec as P


FLOW_STEPS = 4
DIRS = (
    (0, 0, 0),
    (1, 0, 0), (-1, 0, 0), (0, 1, 0), (0, -1, 0), (0, 0, 1), (0, 0, -1),
    (1, 1, 0), (-1, -1, 0), (1, -1, 0), (-1, 1, 0),
    (1, 0, 1), (-1, 0, -1), (1, 0, -1), (-1, 0, 1),
    (0, 1, 1), (0, -1, -1), (0, 1, -1), (0, -1, 1),
)
WEIGHT = (1.0 / 3.0,) + (1.0 / 18.0,) * 6 + (1.0 / 36.0,) * 12
OPP = tuple(DIRS.index(tuple(-v for v in c)) for c in DIRS)
GAIN = (1.0, 0.6, 0.7, 0.35)
HALF = (0.3, 0.5, 0.8, 0.2)
STRIDE = (64, 8, 1)
SITE = np.arange(512)
COORD = np.stack([SITE // 64, SITE // 8 % 8, SITE % 8], axis=1)
UNITS = tuple((a, s) for a in range(3) for s in (1, -1))
UNIT_POPS = tuple(tuple(i for i in range(1, 19) if DIRS[i][a] == s) for a, s in UNITS)
UNIT_SLOT = tuple(
    ((7, 5, 3, 1, 6) if a == 0 else (7, 6, 5, 4, 3))
    if s == 1
    else ((0, 2, 4, 6, 1) if a == 0 else (0, 1, 2, 3, 4))
    for a, s in UNITS
)
F32 = jnp.float32
GRID = (2, 8, 128)


def unit_of(a, s):
    return 2 * a + (0 if s == 1 else 1)


def dir_index(vec):
    return DIRS.index(tuple(vec)) - 1


def edge_unit(i):
    axes = [a for a in range(3) if DIRS[i][a]]
    return axes[1], axes[0]


class Sites:
    def __init__(self):
        sub = lax.broadcasted_iota(jnp.int32, GRID, 1)
        self.lane = lax.broadcasted_iota(jnp.int32, GRID, 2)
        self.sub = sub
        self.coord = (
            (sub & 3) * 2 + (self.lane >> 6),
            (self.lane >> 3) & 7,
            self.lane & 7,
        )
        self.cache = {}

    def plane(self, a, value):
        key = (a, value)
        if key not in self.cache:
            self.cache[key] = self.coord[a] == value
        return self.cache[key]

    def roll(self, v, n, dest):
        low = n % 128
        rows = (n - low) // 128
        lanes = SITE[dest] % 128

        def shift(x, k):
            return pltpu.roll(x, k % 8, 1) if k % 8 else x

        r = pltpu.roll(v, low, 2) if low else v
        same, carried = (lanes >= low).any(), (lanes < low).any()
        if same and carried:
            return jnp.where(self.lane >= low, shift(r, rows), shift(r, rows + 1))
        return shift(r, rows if same else rows + 1)


def moments(f):
    j = []
    for a in range(3):
        t = None
        for i in range(1, 19):
            if DIRS[i][a] == 0:
                continue
            if t is None:
                t = f[i] if DIRS[i][a] == 1 else -f[i]
            else:
                t = t + f[i] if DIRS[i][a] == 1 else t - f[i]
        j.append(t)
    return j


def equilibrium(r, j):
    base = r - 1.5 * (j[0] * j[0] + j[1] * j[1] + j[2] * j[2])
    out = [base * WEIGHT[0]] + [None] * 18
    for i in range(1, 19, 2):
        c = DIRS[i]
        p = None
        for a in range(3):
            if c[a]:
                t = j[a] if c[a] == 1 else -j[a]
                p = t if p is None else p + t
        even = base + 4.5 * (p * p)
        odd = 3.0 * p
        out[i] = WEIGHT[i] * (even + odd)
        out[i + 1] = WEIGHT[i] * (even - odd)
    return out


CODE = 38


def collide_pack(sites, f, relax, post_ref, unit_ref, base=0):
    r = f[0]
    for i in range(1, 19):
        r = r + f[i]
    feq = equilibrium(r, moments(f))
    post = [f[i] - relax * (f[i] - feq[i]) for i in range(19)]
    for i in range(19):
        post_ref[2 * i : 2 * i + 2] = post[i]
    for u, (a, s) in enumerate(UNITS):
        src = 7 if s == 1 else 0
        acc = post[UNIT_POPS[u][0]]
        for i, slot in list(zip(UNIT_POPS[u], UNIT_SLOT[u]))[1:]:
            moved = sites.roll(post[i], (slot - src) * STRIDE[a], COORD[:, a] == slot)
            acc = jnp.where(sites.plane(a, slot), moved, acc)
        unit_ref[base + 2 * u : base + 2 * u + 2] = acc


def stream(sites, me, nbr_ref, post_ref, unit_ref, left_ref, right_ref, code_ref, pool, got, base=0, swapped=True):
    x_even = even("gx")
    for u in range(6):
        left, right = left_ref[2 * u : 2 * u + 2], right_ref[2 * u : 2 * u + 2]
        if swapped:
            left, right = jnp.where(x_even, right, left), jnp.where(x_even, left, right)
        pool[u, 0:16] = left.reshape(16, 128)
        pool[u, 16:32] = unit_ref[base + 2 * u : base + 2 * u + 2].reshape(16, 128)
        pool[u, 32:48] = right.reshape(16, 128)
    first = (me - 1) * 4
    for k in range(18):
        d = DIRS[k + 1]
        i = OPP[k + 1]
        axes = [a for a in range(3) if d[a]]
        a = axes[0] if len(axes) == 1 else edge_unit(i)[0]
        u = unit_of(a, -d[a])
        for b in range(4):
            n = jnp.clip(nbr_ref[0, b, k] - first, 0, 11)
            got[k, 4 * b : 4 * b + 4] = pool[u, pl.ds(pl.multiple_of(4 * n, 4), 4), :]
    eff = code_ref[CODE + 2 : CODE + 4].astype(jnp.int32)
    f = [post_ref[0:2]]
    for i in range(1, 19):
        c = DIRS[i]
        axes = [a for a in range(3) if c[a]]
        dest = {a: (0 if c[a] == 1 else 7) for a in axes}
        at = {a: COORD[:, a] == dest[a] for a in axes}
        shift = sum(c[a] * STRIDE[a] for a in range(3))
        pulled = sites.roll(post_ref[2 * i : 2 * i + 2], shift, ~np.any([at[a] for a in axes], axis=0))
        for a in axes:
            u = unit_of(a, c[a])
            slot = UNIT_SLOT[u][UNIT_POPS[u].index(i)]
            face = [0, 0, 0]
            face[a] = -c[a]
            n = (dest[a] - slot) * STRIDE[a] + shift - c[a] * STRIDE[a]
            where = at[a].copy()
            for o in axes:
                if o != a:
                    where &= ~at[o]
            v = sites.roll(got[dir_index(face)].reshape(GRID), n, where)
            pulled = jnp.where(sites.plane(a, dest[a]), v, pulled)
        if len(axes) == 2:
            a, o = edge_unit(i)
            u = unit_of(a, c[a])
            slot = UNIT_SLOT[u][UNIT_POPS[u].index(i)]
            n = (dest[a] - slot) * STRIDE[a] + (dest[o] - (7 - dest[o])) * STRIDE[o]
            v = sites.roll(got[dir_index([-t for t in c])].reshape(GRID), n, at[a] & at[o])
            both = sites.plane(a, dest[a]) & sites.plane(o, dest[o])
            pulled = jnp.where(both, v, pulled)
        o = OPP[i]
        f.append(jnp.where((eff & (1 << (i - 1))) != 0, pulled, post_ref[2 * o : 2 * o + 2]))
    flag = eff >> 18
    feq = equilibrium(jnp.where(flag == 1, 1.03, 0.97).astype(F32), moments(f))
    edge = flag > 0
    return [jnp.where(edge, feq[i], f[i]) for i in range(19)]


def to_rows(dst, value):
    for r in range(4):
        dst[pl.ds(r, 4, stride=4), :] = value[:, 128 * r : 128 * r + 128]


def slab(field, plane):
    return 12 + 3 * field + plane


def first_kernel(nbr_ref, pop_hbm, visc_hbm, link_hbm, flag_hbm, conc_hbm, diff_hbm, upt_hbm,
                 state, lo, hi,
                 rows, irows, pop_ref, visc_ref, link_ref, flag_in, sem):
    pairs = [(pop_hbm, pop_ref), (visc_hbm, visc_ref), (link_hbm, link_ref), (flag_hbm, flag_in)]
    for out, base in ((lo, 0), (hi, 5)):
        fields = [conc_hbm.at[s] for s in range(4)] + [diff_hbm, upt_hbm]
        for n, field in enumerate(fields):
            pairs.append((field.at[base : base + 3], out.at[slab(n, 0) : slab(n, 3)]))
    copies = [pltpu.make_async_copy(src, dst, sem.at[n]) for n, (src, dst) in enumerate(pairs)]
    for copy in copies:
        copy.start()
    for copy in copies[:4]:
        copy.wait()
    sites = Sites()
    f = []
    for i in range(19):
        to_rows(rows.at[i], pop_ref[i, 0])
    to_rows(rows.at[19], visc_ref[0])
    to_rows(irows.at[0], link_ref[0])
    to_rows(irows.at[1], flag_in[0])
    f = [rows[i].reshape(GRID) * np.float32(WEIGHT[i]) for i in range(19)]
    relax = 1.0 / (3.0 * rows[19].reshape(GRID) + 0.5)
    state[38:40] = relax
    group = lax.broadcasted_iota(jnp.int32, GRID, 0) * 2 + (sites.sub >> 2)
    closed = jnp.zeros(GRID, jnp.int32)
    zero = jnp.zeros(GRID, jnp.int32)
    for k in range(18):
        d = DIRS[k + 1]
        axes = [a for a in range(3) if d[a]]
        if len(axes) == 1:
            a = axes[0]
            s = -d[a]
            bits = jnp.full(GRID, 1 << (OPP[k + 1] - 1), jnp.int32)
            for i in UNIT_POPS[unit_of(a, s)]:
                others = [o for o in range(3) if o != a and DIRS[i][o]]
                if others:
                    o = others[0]
                    off = sites.plane(o, 0 if DIRS[i][o] == 1 else 7)
                    bits = bits | jnp.where(off, 0, 1 << (i - 1))
            bits = jnp.where(sites.plane(a, 0 if s == 1 else 7), bits, 0)
        else:
            i = OPP[k + 1]
            c = DIRS[i]
            a, o = axes
            at = sites.plane(a, 0 if c[a] == 1 else 7) & sites.plane(o, 0 if c[o] == 1 else 7)
            bits = jnp.where(at, 1 << (i - 1), 0)
        gone = [(nbr_ref[0, b, k] < 0).astype(jnp.int32) for b in range(4)]
        miss = jnp.where(
            group < 2,
            jnp.where(group == 0, gone[0], gone[1]),
            jnp.where(group == 2, gone[2], gone[3]),
        )
        closed = closed | jnp.where(miss != 0, bits, zero)
    code = (irows[0].reshape(GRID) & ~closed & ((1 << 18) - 1)) + (irows[1].reshape(GRID) << 18)
    state[40:42] = code.astype(F32)
    collide_pack(sites, f, relax, state, state, CODE + 4)
    lo[0:12] = state[42:54]
    hi[0:12] = state[42:54]
    for copy in copies[4:]:
        copy.wait()


def step_kernel(nbr_ref, state, post_in, unit_in, left_ref, right_ref, post_ref, unit_ref, pool, got):
    sites = Sites()
    me = lax.axis_index("gx")
    f = stream(sites, me, nbr_ref, post_in, unit_in, left_ref, right_ref, state, pool, got)
    collide_pack(sites, f, state[CODE : CODE + 2], post_ref, unit_ref)


def second_kernel(nbr_ref, state, left_ref, right_ref, conc, diff,
                  post_ref, unit_ref, ya, yb, za, zb, pool, got):
    sites = Sites()
    me = lax.axis_index("gx")
    f = stream(sites, me, nbr_ref, state, state, left_ref, right_ref, state, pool, got, CODE + 4, False)
    collide_pack(sites, f, state[CODE : CODE + 2], post_ref, unit_ref)
    first_rims(conc, diff, left_ref, right_ref, ya, yb, za, zb)


def last_kernel(nbr_ref, own_ref, slot_ref, state, post_in, unit_in, left_ref, right_ref, f_ref, send_ref, pool, got, jrows):
    sites = Sites()
    me = lax.axis_index("gx")
    f = stream(sites, me, nbr_ref, post_in, unit_in, left_ref, right_ref, state, pool, got)
    for i in range(19):
        f_ref[i] = f[i].reshape(16, 128)
    j = moments(f)
    for a in range(3):
        v = j[a]
        for bit in (8, 16, 32, 64):
            up = pltpu.roll(v, bit, 2)
            down = up if bit == 64 else pltpu.roll(v, 128 - bit, 2)
            v = jnp.where((sites.lane & bit) != 0, up, down)
        jrows[a] = v.reshape(16, 128)
    send_ref[...] = jnp.zeros(send_ref.shape, F32)
    for b in range(4):
        o = own_ref[0, 4 * me + b]
        for a in range(3):
            for r in range(4):
                send_ref[o, 2 * a + r // 2, r % 2 : r % 2 + 1] = jrows[a, 4 * b + r : 4 * b + r + 1]

        @pl.when(o < 15)
        def _():
            for a in range(3):
                k = 12 + a
                send_ref[o + 1, k // 2, k % 2 : k % 2 + 1] = jrows[a, 4 * b + 3 : 4 * b + 4]

        @pl.when(o > 0)
        def _():
            for a in range(3):
                k = 15 + a
                send_ref[o - 1, k // 2, k % 2 : k % 2 + 1] = jrows[a, 4 * b : 4 * b + 1]


def weighted_kernel(f_ref, out_ref):
    for i in range(19):
        for r in range(4):
            rows = f_ref[i, pl.ds(r, 4, stride=4), :]
            out_ref[i, 0, :, 128 * r : 128 * r + 128] = rows * np.float32(1.0 / WEIGHT[i])


def even(axis):
    return lax.rem(lax.axis_index(axis), 2) == 0


class Rims:
    def __init__(self, lane, ya, yb):
        self.lane, self.ya, self.yb = lane, ya, yb
        self.lo = jnp.zeros((8, 128), F32)
        self.hi = jnp.zeros((8, 128), F32)
        self.y_even = even("gy")

    def put(self, value, j, s, row):
        self.ya[s, row : row + 1] = jnp.where(self.y_even, value[7:8], value[0:1])
        self.yb[s, row : row + 1] = jnp.where(self.y_even, value[0:1], value[7:8])
        at = self.lane == j
        self.lo = jnp.where(at, pltpu.roll(value, j, 1) if j else value, self.lo)
        self.hi = jnp.where(at, pltpu.roll(value, (j + 1) % 128, 1), self.hi)

    def finish(self, za, zb):
        z_even = even("gz")
        za[...] = jnp.where(z_even, self.hi, self.lo)
        zb[...] = jnp.where(z_even, self.lo, self.hi)


def first_rims(conc, diff, xl, xr, ya, yb, za, zb):
    lane = lax.broadcasted_iota(jnp.int32, (8, 128), 1)
    rims = Rims(lane, ya, yb)
    for fld in range(5):
        for p in range(12):
            q = p - 2
            if q < 0:
                v = xl[slab(fld, 3 + q)]
            elif q > 7:
                v = xr[slab(fld, q - 8)]
            else:
                v = conc[fld, q] if fld < 4 else diff[q]
            rims.put(v, fld * 12 + p, fld, p)
    rims.finish(za, zb)


def beside(v, lo, hi, z_lo, z_hi, j):
    sub = lax.broadcasted_iota(jnp.int32, (8, 128), 0)
    lane = lax.broadcasted_iota(jnp.int32, (8, 128), 1)
    ym = jnp.where(sub == 0, jnp.broadcast_to(lo, (8, 128)), pltpu.roll(v, 1, 0))
    yp = jnp.where(sub == 7, jnp.broadcast_to(hi, (8, 128)), pltpu.roll(v, 7, 0))
    return (ym, yp) + beside_z(v, z_lo, z_hi, j, j)


def beside_z(v, z_lo, z_hi, j_lo, j_hi):
    lane = lax.broadcasted_iota(jnp.int32, (8, 128), 1)
    zm = jnp.where(lane == 0, turn(z_lo, -j_lo), pltpu.roll(v, 1, 1))
    zp = jnp.where(lane == 127, turn(z_hi, 127 - j_hi), pltpu.roll(v, 127, 1))
    return zm, zp


def turn(v, n):
    return pltpu.roll(v, n % 128, 1) if n % 128 else v


def advance(s, cm, c, cp, around, spread, drift, upt, up1):
    k = GAIN[s]
    acc = c
    for v, g, d in zip((cm, cp) + tuple(around), spread, drift):
        w = d + (g if k == 1.0 else k * g)
        acc = acc + w * (v - c)
    if s == 2:
        return acc + 2.0 * up1
    return acc - upt * c / (HALF[s] + jnp.abs(c))


def tissue(lo, hi, get_c, around, get_coef, get_upt, me, store):
    for p in range(lo, hi):
        spread, drift = get_coef(p)
        upt = get_upt(p)
        keep = me > 0 if p < 0 else (me < 15 if p > 7 else None)
        c1 = get_c(1, p)
        up1 = upt * c1 / (HALF[1] + jnp.abs(c1))
        for s in range(4):
            c = get_c(s, p)
            v = advance(s, get_c(s, p - 1), c, get_c(s, p + 1), around(s, p, c), spread, drift, upt, up1)
            if keep is not None:
                v = jnp.where(keep, v, 0.0)
            store(s, p, v)


def place_velocity(own_ref, slot_ref, recv, drift, blocks, slabs):
    me = lax.axis_index("gx")
    blocks[...] = jnp.zeros(blocks.shape, F32)
    slabs[...] = jnp.zeros(slabs.shape, F32)
    for m in range(16):
        own, low, high = jnp.int32(16), jnp.int32(16), jnp.int32(16)
        for b in range(4):
            o = own_ref[0, 4 * m + b]
            at = slot_ref[0, 4 * m + b]
            own = jnp.where(o == me, at, own)
            low = jnp.where(o == me - 1, at, low)
            high = jnp.where(o == me + 1, at, high)
        for k in range(18):
            row = recv[m, k // 2, k % 2 : k % 2 + 1]
            if k < 12:
                blocks[pl.ds(16 * own + k, 1), :] = row
            else:
                slabs[k - 12, pl.ds(low if k < 15 else high, 1), :] = row
    group = lax.broadcasted_iota(jnp.int32, (16, 128), 1) >> 3
    masks = [(group & (1 << bit)) != 0 for bit in range(4)]

    def turned(x):
        x = pltpu.roll(x, 8, 1, stride=8, stride_axis=0)
        for bit in range(4):
            x = jnp.where(masks[bit], pltpu.roll(x, 16 - (1 << bit), 0), x)
        return pltpu.roll(x, 0, 1, stride=8, stride_axis=0)

    for a in range(3):
        for r in range(6):
            if r == 0:
                x = slabs[a, 0:16]
            elif r == 5:
                x = slabs[3 + a, 0:16]
            else:
                x = blocks[pl.ds(4 * a + r - 1, 16, stride=16), :]
            t = turned(x)
            for h in range(2):
                u = 3.0 * t[8 * h : 8 * h + 8]
                drift[2 * a, 2 * r + h] = jnp.maximum(u, 0.0)
                drift[2 * a + 1, 2 * r + h] = -jnp.minimum(u, 0.0)


NEXT, COEF, FACE_ROWS = 64, 96, 176


def brick_field(xl, xr, f, own):
    def get(p):
        if p < 0:
            return xl[slab(f, 3 + p)]
        if p > 7:
            return xr[slab(f, p - 8)]
        return own(p)

    return get


def first_around(za, zb, ya, yb):
    y_even, z_even = even("gy"), even("gz")
    z_lo = jnp.where(z_even, zb[...], za[...])
    z_hi = jnp.where(z_even, za[...], zb[...])

    def around(s, p, c):
        a, b = ya[s, p + 2 : p + 3], yb[s, p + 2 : p + 3]
        lo, hi = jnp.where(y_even, b, a), jnp.where(y_even, a, b)
        return beside(c, lo, hi, z_lo, z_hi, 12 * s + p + 2)

    return around


def put_rows(ma, mb, y_even, row, low, high):
    ma[row : row + 1] = jnp.where(y_even, high, low)
    mb[row : row + 1] = jnp.where(y_even, low, high)


def put_lanes(pair, j, value, depth):
    at = lax.broadcasted_iota(jnp.int32, (8, 128), 1) == j
    pair[0] = jnp.where(at, turn(value, j - depth), pair[0])
    pair[1] = jnp.where(at, turn(value, j - 127 + depth), pair[1])


def spread_kernel(conc, diff, upt, xl, xr, za, zb, ya, yb, part, spread_out, ca, cb, coef_lo, coef_hi):
    y_even = even("gy")
    around = first_around(za, zb, ya, yb)
    coefs = [jnp.zeros((8, 128), F32)] * 2
    get_d = brick_field(xl, xr, 4, lambda p: diff[p])
    get_u = brick_field(xl, xr, 5, lambda p: upt[p])
    gets = [brick_field(xl, xr, s, lambda p, s=s: conc[s, p]) for s in range(4)]
    for p in range(-2, 10):
        d, u = get_d(p), get_u(p)
        spread = [0.5 * (d + n) for n in (get_d(p - 1), get_d(p + 1)) + around(4, p, d)]
        for n in range(6):
            spread_out[n, p + 2] = spread[n]
        if 0 <= p < 8:
            for n, v in enumerate(spread + [u]):
                put_rows(ca, cb, y_even, 8 * n + p, v[0:1], v[7:8])
                put_lanes(coefs, 8 * n + p, v, 0)
        c1 = gets[1](p)
        up1 = u * c1 / (HALF[1] + jnp.abs(c1))
        for s in range(4):
            c = gets[s](p)
            total = None
            for g, v in zip(spread, (gets[s](p - 1), gets[s](p + 1)) + around(s, p, c)):
                t = g * (v - c)
                total = t if total is None else total + t
            v = c + GAIN[s] * total
            part[s, p + 2] = v + 2.0 * up1 if s == 2 else v - u * c / (HALF[s] + jnp.abs(c))
    coef_lo[...] = coefs[0]
    coef_hi[...] = coefs[1]


def drift_kernel(own_ref, slot_ref, recv, part, conc, xl, xr, za, zb, ya, yb, ca, cb, coef_lo_in, coef_hi_in,
                 drift, c_out, ma, mb, pack_lo, pack_hi, coef_lo, coef_hi, blocks, slabs):
    me = lax.axis_index("gx")
    y_even = even("gy")
    place_velocity(own_ref, slot_ref, recv, drift, blocks, slabs)
    around = first_around(za, zb, ya, yb)
    gets = [brick_field(xl, xr, s, lambda p, s=s: conc[s, p]) for s in range(4)]
    packs = [jnp.zeros((8, 128), F32)] * 2
    coefs = [coef_lo_in[...], coef_hi_in[...]]
    ma[0:COEF] = jnp.zeros((COEF, 128), F32)
    mb[0:COEF] = jnp.zeros((COEF, 128), F32)
    ma[COEF : COEF + 56] = ca[...]
    mb[COEF : COEF + 56] = cb[...]
    for p in range(-2, 10):
        flow = [drift[n, p + 2] for n in range(6)]
        if 0 <= p < 8:
            for a in range(3):
                v = flow[2 * a] - flow[2 * a + 1]
                put_rows(ma, mb, y_even, COEF + 8 * (7 + a) + p, v[0:1], v[7:8])
                put_lanes(coefs, 8 * (7 + a) + p, v, 0)
        keep = me > 0 if p < 0 else (me < 15 if p > 7 else None)
        for s in range(4):
            c = gets[s](p)
            v = part[s, p + 2]
            for d, n in zip(flow, (gets[s](p - 1), gets[s](p + 1)) + around(s, p, c)):
                v = v + d * (n - c)
            if keep is not None:
                v = jnp.where(keep, v, 0.0)
            c_out[s, p + 2] = v
            if -1 <= p < 9:
                put_rows(ma, mb, y_even, 16 * s + p + 1, v[0:1], v[7:8])
                put_lanes(packs, 10 * s + p + 1, v, 0)
            if 0 <= p < 8:
                put_rows(ma, mb, y_even, NEXT + 8 * s + p, v[1:2], v[6:7])
                put_lanes(packs, 40 + 8 * s + p, v, 1)
    pack_lo[...] = packs[0]
    pack_hi[...] = packs[1]
    coef_lo[...] = coefs[0]
    coef_hi[...] = coefs[1]


class Faces:
    def __init__(self, a, b):
        self.a, self.b, self.y_even = a, b, even("gy")

    def rows(self, side, start, count):
        a, b = self.a[start : start + count], self.b[start : start + count]
        return jnp.where(self.y_even, b, a) if side == 0 else jnp.where(self.y_even, a, b)


def corner_kernel(ya, yb, pack_lo, pack_hi, coef_lo, coef_hi, za, zb):
    lane = lax.broadcasted_iota(jnp.int32, (8, 128), 1)
    faces = Faces(ya, yb)
    corners = [jnp.zeros((8, 128), F32)] * 2
    for side in range(2):
        for s in range(4):
            v = faces.rows(side, 16 * s + 1, 8)
            at = lane == 4 * side + s
            corners[0] = jnp.where(at, turn(v, 4 * side + s), corners[0])
            corners[1] = jnp.where(at, turn(v, 4 * side + s - 127), corners[1])
    z_even = even("gz")
    low = (pack_lo[...], coef_lo[...], corners[0])
    high = (pack_hi[...], coef_hi[...], corners[1])
    for n in range(3):
        za[n] = jnp.where(z_even, high[n], low[n])
        zb[n] = jnp.where(z_even, low[n], high[n])


def tissue23_kernel(drift, spread, conc, upt, xl, xr, ya, yb, ma, mb, pack_lo, pack_hi, za, zb,
                    out, mid, y_face):
    me = lax.axis_index("gx")
    sub = lax.broadcasted_iota(jnp.int32, (8, 128), 0)
    lane = lax.broadcasted_iota(jnp.int32, (8, 128), 1)
    got, sent = Faces(ya, yb), Faces(ma, mb)
    z_even = even("gz")
    low = [jnp.where(z_even, zb[n], za[n]) for n in range(3)]
    high = [jnp.where(z_even, za[n], zb[n]) for n in range(3)]

    def flows(u):
        parts = []
        for v in u:
            parts += [jnp.maximum(v, 0.0), -jnp.minimum(v, 0.0)]
        return parts

    for side in range(2):
        coef = [got.rows(side, COEF + 8 * n, 8) for n in range(10)]
        cs = [got.rows(side, 16 * s + 1, 8) for s in range(4)]
        up1 = coef[6] * cs[1] / (HALF[1] + jnp.abs(cs[1]))
        for s in range(4):
            inner = sent.rows(side, 16 * s + 1, 8)
            outer = got.rows(side, NEXT + 8 * s, 8)
            j = 4 * side + s
            around = ((outer, inner) if side == 0 else (inner, outer)) + beside_z(cs[s], low[2], high[2], j, j)
            y_face[side, s] = advance(
                s, got.rows(side, 16 * s, 8), cs[s], got.rows(side, 16 * s + 2, 8), around,
                coef[:6], flows(coef[7:10]), coef[6], up1,
            )
    z_face = []
    for side, (pack, own) in enumerate(((low, pack_lo[...]), (high, pack_hi[...]))):
        coef = [turn(pack[1], -8 * n) for n in range(10)]
        flow = flows(coef[7:10])
        cs = [turn(pack[0], -(10 * s + 1)) for s in range(4)]
        up1 = coef[6] * cs[1] / (HALF[1] + jnp.abs(cs[1]))
        for s in range(4):
            edge = []
            for y_side in range(2):
                j = 4 * y_side + s
                column = jnp.broadcast_to(pack[2][:, j : j + 1], (8, 128))
                edge.append(jnp.sum(jnp.where(sub == lane, column, 0.0), axis=0, keepdims=True))
            ym = jnp.where(sub == 0, jnp.broadcast_to(edge[0], (8, 128)), pltpu.roll(cs[s], 1, 0))
            yp = jnp.where(sub == 7, jnp.broadcast_to(edge[1], (8, 128)), pltpu.roll(cs[s], 7, 0))
            inner, outer = turn(own, -(10 * s + 1)), turn(pack[0], -(40 + 8 * s))
            around = (ym, yp) + ((outer, inner) if side == 0 else (inner, outer))
            z_face.append(advance(
                s, turn(pack[0], -10 * s), cs[s], turn(pack[0], -(10 * s + 2)), around,
                coef[:6], flow, coef[6], up1,
            ))

    def get_u(p):
        return xl[slab(5, 3 + p)] if p < 0 else (xr[slab(5, p - 8)] if p > 7 else upt[p])

    def get_coef(p):
        return [spread[n, p + 2] for n in range(6)], [drift[n, p + 2] for n in range(6)]

    def around2(s, p, c):
        q = p + 1
        lo, hi = got.rows(0, 16 * s + q, 1), got.rows(1, 16 * s + q, 1)
        return beside(c, lo, hi, low[0], high[0], 10 * s + q)

    def store2(s, p, v):
        mid[s, p + 1] = v

    tissue(-1, 9, lambda s, p: conc[s, p + 2], around2, get_coef, get_u, me, store2)

    def around3(s, p, c):
        lo, hi = y_face[0, s, p : p + 1], y_face[1, s, p : p + 1]
        return beside(c, lo, hi, z_face[s], z_face[4 + s], p)

    def store3(s, p, v):
        out[s, p] = v

    tissue(0, 8, lambda s, p: mid[s, p + 1], around3, get_coef, get_u, me, store3)


VMEM = pltpu.VMEM


def call(kernel, smem, arrays, outs, scratch=(), space=VMEM, limit=8 << 20):
    return pl.pallas_call(
        kernel,
        in_specs=[pl.BlockSpec(memory_space=pltpu.SMEM)] * len(smem)
        + [pl.BlockSpec(memory_space=space)] * len(arrays),
        out_specs=tuple(pl.BlockSpec(memory_space=VMEM) for _ in outs),
        out_shape=tuple(jax.ShapeDtypeStruct(s, t) for s, t in outs),
        scratch_shapes=[VMEM(*x) if isinstance(x, tuple) else x for x in scratch],
        compiler_params=pltpu.CompilerParams(vmem_limit_bytes=limit),
    )(*smem, *arrays)


def hop(x, axis, step):
    n = lax.axis_size(axis)
    return lax.ppermute(x, axis, [(i, i + step) for i in range(n) if 0 <= i + step < n])


def swap(x, axis, first):
    n = lax.axis_size(axis)
    return lax.ppermute(x, axis, [(i, j) for i in range(n) for j in [i ^ 1 if first else ((i + 1) ^ 1) - 1] if 0 <= j < n])


def swaps(ya, yb, za, zb):
    out = []
    for x, axis, first in ((za, "gz", True), (zb, "gz", False), (ya, "gy", True), (yb, "gy", False)):
        out.append(swap(x, axis, first))
    return tuple(out)


def program(populations, viscosity, links, flags, neighbours, owners, slots, conc, diff, upt):
    i32 = jnp.int32
    tiles = lambda n: ((n, 8, 128), F32)
    tile = ((8, 128), F32)
    faces = lambda fields, rows: [((fields, rows, 128), F32)] * 2 + [tile, tile]
    pool = [((6, 48, 128), F32), ((18, 16, 128), F32)]
    state, lo, hi = call(
        first_kernel, (neighbours,), (populations, viscosity, links, flags, conc, diff, upt),
        [tiles(54), tiles(30), tiles(30)],
        [((20, 16, 128), F32), ((2, 16, 128), i32), ((19, 1, 4, 512), F32), ((1, 4, 512), F32),
         ((1, 4, 512), i32), ((1, 4, 512), i32), pltpu.SemaphoreType.DMA((16,))],
        space=pltpu.HBM, limit=67043328 - (420 << 10),
    )
    xl, xr = hop(hi, "gx", 1), hop(lo, "gx", -1)
    post, unit, *rim = call(
        second_kernel, (neighbours,), (state, xl, xr, conc, diff),
        [tiles(38), tiles(12)] + faces(5, 16), pool,
    )
    rim = swaps(*rim)
    for _ in range(FLOW_STEPS - 2):
        left, right = swap(unit, "gx", True), swap(unit, "gx", False)
        post, unit = call(
            step_kernel, (neighbours,), (state, post, unit, left, right), [tiles(38), tiles(12)], pool
        )
    left, right = swap(unit, "gx", True), swap(unit, "gx", False)
    last, send = call(
        last_kernel, (neighbours, owners, slots), (state, post, unit, left, right),
        [((19, 16, 128), F32), ((16, 9, 2, 128), F32)], pool + [((3, 16, 128), F32)],
    )
    recv = lax.all_to_all(send, "gx", 0, 0)
    (weighted,) = call(weighted_kernel, (), (last,), [((19, 1, 4, 512), F32)])
    face = ((FACE_ROWS, 128), F32)
    twelve = lambda n: ((n, 12, 8, 128), F32)
    part, spread, ca, cb, coef_lo, coef_hi = call(
        spread_kernel, (), (conc, diff, upt, xl, xr) + rim,
        [twelve(4), twelve(6), ((56, 128), F32), ((56, 128), F32), tile, tile],
    )
    drift, c1, ma, mb, pack_lo, pack_hi, coef_lo, coef_hi = call(
        drift_kernel, (owners, slots), (recv, part, conc, xl, xr) + rim + (ca, cb, coef_lo, coef_hi),
        [twelve(6), twelve(4), face, face] + [tile] * 4,
        [((17 * 16, 128), F32), ((6, 24, 128), F32)],
    )
    ya = swap(ma, "gy", True)
    yb = swap(mb, "gy", False)
    za, zb = call(
        corner_kernel, (), (ya, yb, pack_lo, pack_hi, coef_lo, coef_hi), [tiles(3), tiles(3)]
    )
    za, zb = swap(za, "gz", True), swap(zb, "gz", False)
    (out,) = call(
        tissue23_kernel, (),
        (drift, spread, c1, upt, xl, xr, ya, yb, ma, mb, pack_lo, pack_hi, za, zb),
        [((4, 8, 8, 128), F32)], [((4, 10, 8, 128), F32), ((2, 4, 8, 128), F32)],
    )
    return weighted, out


def solution(mesh):
    site = P(("gy", "gz"), "gx", None)
    brick = P("gx", "gy", "gz")
    return jax.shard_map(
        program,
        mesh=mesh,
        in_specs=(
            P(None, ("gy", "gz"), "gx", None), site, site, site, site,
            P(("gy", "gz"), None), P(("gy", "gz"), None),
            P(None, "gx", "gy", "gz"), brick, brick,
        ),
        out_specs=(P(None, ("gy", "gz"), "gx", None), P(None, "gx", "gy", "gz")),
        check_vma=False,
    )
```
